512 devices in a mesh: grp: 16 (over z), dev: 32 (over y, x, core).
Axes of the slice: x: 4, y: 4, z: 16, core: 2. Of those that a mesh axis runs over, the one named last changes fastest.
Arguments:
- particles: bfloat16 [8192, 2, 6144], P(('grp', 'dev')), may hold values from -24 to 24
- defocus_bin: int32 [8192], P(('grp', 'dev')), may hold values from 0 to 15
- candidates: int32 [8192, 8], P(('grp', 'dev')), may hold values from 0 to 63, as said below
- projections: bfloat16 [64, 2, 6144], P('dev'), may hold values from -1 to 1
- ctf_table: bfloat16 [16, 6144], replicated, may hold values from -1 to 1
- inv_noise: float32 [6144], replicated, may hold values from 0.25 to 4
- line_slab: int32 [64, 48], P('dev'), may hold values from 0 to 15, as said below
- slab_owner: int32 [16], replicated, may hold values from 0 to 15, each once
Outputs:
- slab_data: float32 [16, 64, 2, 6, 128], P('grp', 'dev')
- slab_weight: float32 [16, 64, 6, 128], P('grp', 'dev')
The draws below stay inside these ranges and needn't reach their ends.
Inputs may be any that keep to these rules, and one draw needn't show every extreme that they name: `candidates`: each particle lists 8 different projections. `line_slab`: no slab holds more than 6 lines of one projection, and for every projection one slab holds exactly 6 of them. `slab_owner`: each group owns exactly one slab.
All inputs are finite; a program needn't handle non-finite values.
Results may differ from the reference program's by a relative error of at most 0.02.
Values may be sent and summed in bfloat16 or wider, within the bound.
A program may use at most 64 MiB of HBM per device.

```python
import math
import jax
import jax.numpy as jnp
from jax import lax

LINE_LEN = 128
NUM_LINES = 48
PIXELS = 6144
PART_DEV = 16
PARTICLES = 8192
PROJECTIONS = 64
SHIFTS = 9
CANDIDATES = 8
DEFOCUS_BINS = 16
SLABS = 16
CAPACITY = 6
N_GRP = 16
N_DEV = 32


def projection_scales(key):
    spread = jax.random.uniform(jax.random.fold_in(key, 102), (PROJECTIONS,), jnp.float32, math.log(0.5), math.log(2.0))
    return jnp.exp(spread)


def projection_values(key):
    base = jax.random.fold_in(key, 101)
    shape = (PROJECTIONS, 2, PIXELS)
    values = jnp.clip(jax.random.normal(base, shape, jnp.float32), -5.0, 5.0)
    amplitude = projection_scales(key)
    return values * amplitude[:, None, None] * (1.0 / math.sqrt(PIXELS))


def ctf_values(key):
    values = jax.random.uniform(jax.random.fold_in(key, 202), (DEFOCUS_BINS, PIXELS), jnp.float32, -1.0, 1.0)
    return values


def bin_values(key):
    return jax.random.randint(jax.random.fold_in(key, 303), (PARTICLES,), 0, DEFOCUS_BINS, dtype=jnp.int32)


def candidate_values(key):
    raw_scores = jax.random.randint(jax.random.fold_in(key, 404), (PARTICLES, PROJECTIONS), 0, 1 << 20, dtype=jnp.int32)
    raw_scores = raw_scores * PROJECTIONS + jnp.arange(PROJECTIONS, dtype=jnp.int32)[None, :]
    picked = lax.top_k(raw_scores, CANDIDATES)[1]
    return picked.astype(jnp.int32)


def draw_projections(key, part):
    return projection_values(key).astype(jnp.bfloat16)


def draw_ctf_table(key, part):
    return ctf_values(key).astype(jnp.bfloat16)


def draw_defocus_bin(key, part):
    return bin_values(key)


def draw_candidates(key, part):
    return candidate_values(key)


def draw_particles(key, part):
    base = jax.random.fold_in(key, 505)
    shape = (PARTICLES, 2, PIXELS)
    noise = jax.random.normal(base, shape, jnp.float32)
    return jnp.clip(noise, -24.0, 24.0).astype(jnp.bfloat16)


def draw_line_slab(key, part):
    row_keys = jax.random.split(jax.random.fold_in(key, 606), PROJECTIONS)

    def one_row(row_key):
        pick_key, mix_key, order_key = jax.random.split(row_key, 3)
        hottest = jax.random.randint(pick_key, (), 0, SLABS, dtype=jnp.int32)
        label_pool = jnp.arange(SLABS * CAPACITY, dtype=jnp.int32) // CAPACITY
        others = jax.random.permutation(mix_key, label_pool[CAPACITY:])[:NUM_LINES - CAPACITY]
        labels = jnp.concatenate([jnp.zeros((CAPACITY,), jnp.int32), others])
        labels = (labels + hottest) % SLABS
        return jax.random.permutation(order_key, labels)
    return jax.vmap(one_row)(row_keys)


def setup_inputs(seed: int = 0) -> dict:
    arg_keys = jax.random.split(jax.random.key(seed), 9)
    return {
        "particles": draw_particles(jax.random.fold_in(arg_keys[8], 71), 0),
        "defocus_bin": draw_defocus_bin(jax.random.fold_in(arg_keys[8], 71), 0),
        "candidates": draw_candidates(jax.random.fold_in(arg_keys[8], 71), 0),
        "projections": draw_projections(jax.random.fold_in(arg_keys[8], 71), 0),
        "ctf_table": draw_ctf_table(jax.random.fold_in(arg_keys[8], 71), 0),
        "inv_noise": jnp.clip(jnp.exp(jax.random.uniform(arg_keys[5], (PIXELS,), jnp.float32, math.log(0.25), math.log(4.0))), 0.25, 4.0),
        "line_slab": draw_line_slab(jax.random.fold_in(arg_keys[8], 71), 0),
        "slab_owner": jax.random.permutation(arg_keys[7], SLABS).astype(jnp.int32),
    }


two_pi = 2.0 * math.pi
exact = lax.Precision.HIGHEST


def phase_tables():
    pixel_index = jnp.arange(PIXELS, dtype=jnp.int32)
    line_pos = (pixel_index // LINE_LEN).astype(jnp.float32)
    column = pixel_index % LINE_LEN
    frequency = jnp.where(column < LINE_LEN // 2, column, column - LINE_LEN).astype(jnp.float32)
    shift_index = jnp.arange(SHIFTS, dtype=jnp.int32)
    move_x = (shift_index // 3 - 1).astype(jnp.float32)
    move_y = (shift_index % 3 - 1).astype(jnp.float32)
    angles = (move_x[:, None] * line_pos[None, :] + move_y[:, None] * frequency[None, :]) * (two_pi / LINE_LEN)
    return jnp.cos(angles), jnp.sin(angles)


def slot_tables(line_slab, slab_owner):
    slab_ids = jnp.arange(SLABS, dtype=jnp.int32)
    slab_hit = line_slab[:, :, None] == slab_ids[None, None, :]
    owner_line = jnp.sum(jnp.where(slab_hit, slab_owner[None, None, :], 0), axis=2).astype(jnp.int32)
    line_ids = jnp.arange(NUM_LINES, dtype=jnp.int32)
    earlier = line_ids[None, :] < line_ids[:, None]
    same_owner = owner_line[:, :, None] == owner_line[:, None, :]
    line_rank = jnp.sum(jnp.logical_and(same_owner, earlier[None]), axis=2).astype(jnp.int32)
    return owner_line, line_rank


def reference(particles, defocus_bin, candidates, projections, ctf_table, inv_noise, line_slab, slab_owner):
    cosines, sine_table = phase_tables()
    table_values = ctf_table.astype(jnp.float32)
    ctf_square = table_values * table_values
    noisy_square = ctf_square * inv_noise[None, :]
    proj_values = projections.astype(jnp.float32)
    pix_power = proj_values[:, 0] * proj_values[:, 0] + proj_values[:, 1] * proj_values[:, 1]
    bin_power = jnp.dot(noisy_square, pix_power.T, precision=exact)
    real_shift = proj_values[None, :, 0] * cosines[:, None, :] - proj_values[None, :, 1] * sine_table[:, None, :]
    imag_shift = proj_values[None, :, 0] * sine_table[:, None, :] + proj_values[None, :, 1] * cosines[:, None, :]
    shifted = jnp.concatenate([real_shift, imag_shift], axis=2)
    shifted = lax.optimization_barrier(shifted.astype(jnp.bfloat16)).astype(jnp.float32)

    blocks = N_GRP * N_DEV
    device_blocks = particles.reshape(blocks, PART_DEV, 2, PIXELS)
    bin_blocks = defocus_bin.reshape(blocks, PART_DEV)
    cand_blocks = candidates.reshape(blocks, PART_DEV, CANDIDATES)
    proj_ids = jnp.arange(PROJECTIONS, dtype=jnp.int32)
    bin_ids = jnp.arange(DEFOCUS_BINS, dtype=jnp.int32)

    def one_device(carry, inputs):
        data_sum, bin_sum = carry
        block, block_bins, block_cands = inputs
        onehot = (block_bins[:, None] == bin_ids[None, :]).astype(jnp.float32)
        ctf_rows = jnp.dot(onehot, table_values, precision=exact)
        images = block.astype(jnp.float32)
        weighted = (inv_noise[None, :] * ctf_rows)[:, None, :] * images
        weighted = lax.optimization_barrier(weighted.astype(jnp.bfloat16)).astype(jnp.float32)
        weighted = weighted.reshape(PART_DEV, 2 * PIXELS)
        scored = jnp.einsum("ik,tjk->itj", weighted, shifted, precision=exact)
        quad_term = jnp.dot(onehot, bin_power, precision=exact)
        scores = scored - 0.5 * quad_term[:, None, :]
        listed = jnp.any(block_cands[:, :, None] == proj_ids[None, None, :], axis=1)
        masked = jnp.where(listed[:, None, :], scores, -jnp.inf)
        row_peak = jnp.max(masked, axis=(1, 2), keepdims=True)
        exp_terms = jnp.exp(masked - row_peak)
        posterior = exp_terms / jnp.sum(exp_terms, axis=(1, 2), keepdims=True)
        post_low = lax.optimization_barrier(posterior.astype(jnp.bfloat16)).astype(jnp.float32)
        ctf_image = ctf_rows[:, None, :] * images
        ctf_image = lax.optimization_barrier(ctf_image.astype(jnp.bfloat16)).astype(jnp.float32)
        ctf_image = ctf_image.reshape(PART_DEV, 2 * PIXELS)
        summed = jnp.einsum("itj,ik->tjk", post_low, ctf_image, precision=exact)
        real_sum = summed[:, :, :PIXELS]
        imag_sum = summed[:, :, PIXELS:]
        data_real = jnp.sum(real_sum * cosines[:, None, :] + imag_sum * sine_table[:, None, :], axis=0)
        data_imag = jnp.sum(imag_sum * cosines[:, None, :] - real_sum * sine_table[:, None, :], axis=0)
        device_slice = jnp.stack([data_real, data_imag], axis=1)
        device_slice = lax.optimization_barrier(device_slice.astype(jnp.bfloat16)).astype(jnp.float32)
        proj_share = jnp.sum(posterior, axis=1)
        bin_share = jnp.dot(proj_share.T, onehot, precision=exact)
        return (data_sum + device_slice, bin_sum + bin_share), None

    start_data = jnp.zeros((PROJECTIONS, 2, PIXELS), jnp.float32)
    start_bins = jnp.zeros((PROJECTIONS, DEFOCUS_BINS), jnp.float32)
    (slice_data, bin_total), _ = lax.scan(one_device, (start_data, start_bins), (device_blocks, bin_blocks, cand_blocks))
    slice_weight = jnp.dot(bin_total, ctf_square, precision=exact) * (PROJECTIONS / PARTICLES)

    data_lines = slice_data.reshape(PROJECTIONS, 2, NUM_LINES, LINE_LEN)
    weight_lines = slice_weight.reshape(PROJECTIONS, NUM_LINES, LINE_LEN)
    owner_line, line_rank = slot_tables(line_slab, slab_owner)
    group_ids = jnp.arange(SLABS, dtype=jnp.int32)
    slot_ids = jnp.arange(CAPACITY, dtype=jnp.int32)
    selector = jnp.logical_and(owner_line[None, :, None, :] == group_ids[:, None, None, None], line_rank[None, :, None, :] == slot_ids[None, None, :, None]).astype(jnp.float32)
    slab_data = jnp.einsum("ojcl,jxlp->ojxcp", selector, data_lines, precision=exact)
    slab_weight = jnp.einsum("ojcl,jlp->ojcp", selector, weight_lines, precision=exact)
    return slab_data, slab_weight
```

```python
import math

import jax
import jax.numpy as jnp
import numpy as np
from jax import lax
from jax.experimental import pallas as pl
from jax.experimental.pallas import tpu as pltpu
from jax.sharding import PartitionSpec as P

LINE = 128
CAP = 6
BINS = 16
NODES = 16
COLOURS = 4
ROWS = 8
NEG = -3.0e38
MESH = pl.DeviceIdType.MESH
F32 = jnp.float32
BF16 = jnp.bfloat16
HIGH = lax.Precision.HIGHEST
NN = (((1,), (0,)), ((), ()))
NT = (((1,), (1,)), ((), ()))
TN = (((0,), (0,)), ((), ()))
STEPS = (1, 3, 4, 12)


def dot(a, b, dims=NN, precision=None):
    return lax.dot_general(a, b, dims, preferred_element_type=F32, precision=precision)


def phase_rows(lines):
    line = np.repeat(np.arange(lines), LINE).astype(np.float64)
    column = np.tile(np.arange(LINE), lines)
    freq = np.where(column < LINE // 2, column, column - LINE).astype(np.float64)
    moves = ((0, 1), (1, -1), (1, 0), (1, 1))
    angle = np.stack([dx * line + dy * freq for dx, dy in moves]) * (2.0 * math.pi / LINE)
    return np.concatenate([np.cos(angle), np.sin(angle)]).astype(np.float32)


def offset_of(colour, mask):
    off = 0
    for p in range(4):
        if mask >> p & 1:
            off ^= STEPS[(p + colour) % 4]
    return off


def flip(v, k):
    if k == 0:
        return v
    if k == 1:
        return v + 1 - 2 * (v % 2)
    if k == 2:
        return (v + 2) % 4
    return 3 - v


def top(mask):
    return mask.bit_length() - 1


def make_kernel(lines, groups):
    half = lines * LINE // 2
    width = half // COLOURS
    hl = lines // 2
    slots = 32

    def kernel(parts, proj, table, noise, trig, cand, bins, slab, owner,
               o_data, o_weight,
               xin, pin, candb, binb, trigv, tabh, tabf, noisev, asm, pbuf, rbuf, gscr, bpscr, sx,
               cscr, bsscr, dbuf, rsb, zb, sel, wkey, w3, zsend, zrecv, wzs, wzr,
               loc, ex_s, ex_r, ag_s, ag_r, rs_s, rs_r, sx_sem, zx_sem, z_s, z_r, w_s, w_r):
        z = lax.axis_index("grp")
        d = lax.axis_index("dev")
        core = d % 2
        node = d // 2
        nx, ny = node % 4, node // 4
        other = 1 - core

        def at(k):
            return flip(ny, k // 4) * 4 + flip(nx, k % 4)

        def dev(k):
            return (z, at(k) * 2 + core)

        mate = (z, node * 2 + other)

        barrier = pltpu.get_barrier_semaphore()
        pl.semaphore_signal(barrier, inc=1, device_id=mate, device_id_type=MESH)
        for k in STEPS:
            pl.semaphore_signal(barrier, inc=1, device_id=dev(k), device_id_type=MESH)
        for k in range(1, groups):
            pl.semaphore_signal(barrier, inc=1, device_id=((z + k) % groups, d), device_id_type=MESH)

        mine = pl.ds(pl.multiple_of(core * half, LINE), half)
        theirs = pl.ds(pl.multiple_of(other * half, LINE), half)
        loads = [
            pltpu.make_async_copy(proj.at[:, :, mine], pin.at[core], loc.at[0]),
            pltpu.make_async_copy(parts.at[:, :, mine], xin.at[core], loc.at[1]),
            pltpu.make_async_copy(table.at[:, mine], tabh, loc.at[2]),
            pltpu.make_async_copy(trig.at[:, mine], trigv, loc.at[3]),
            pltpu.make_async_copy(noise.at[:, mine], noisev, loc.at[4]),
            pltpu.make_async_copy(table, tabf, loc.at[5]),
            pltpu.make_async_copy(cand, candb.at[core], loc.at[6]),
            pltpu.make_async_copy(bins, binb.at[core], loc.at[7]),
        ]
        for c in loads:
            c.start()

        lanes = lax.broadcasted_iota(jnp.int32, (1, 128), 1)
        lid = lax.broadcasted_iota(jnp.int32, (groups, lines), 0)
        tri = (
            lax.broadcasted_iota(jnp.int32, (lines, lines), 0)
            < lax.broadcasted_iota(jnp.int32, (lines, lines), 1)
        ).astype(F32)
        wide = (
            lax.broadcasted_iota(jnp.int32, (lines, lines * ROWS), 1) // ROWS
            == lax.broadcasted_iota(jnp.int32, (lines, lines * ROWS), 0)
        ).astype(F32)
        wide16 = (
            lax.broadcasted_iota(jnp.int32, (lines, lines * BINS), 1) // BINS
            == lax.broadcasted_iota(jnp.int32, (lines, lines * BINS), 0)
        ).astype(F32)
        keys = []
        for j in range(2):
            row = slab[j : j + 1, :]
            own = jnp.zeros((1, lines), jnp.int32)
            for s in range(groups):
                own = own + jnp.where(row == s, owner[s], 0)
            hit = (lid == own).astype(F32)
            rank = jnp.sum(hit * dot(hit, tri), axis=0, keepdims=True)
            keys.append((own * 8).astype(F32) + rank)
        key8 = [dot(k, wide) for k in keys]
        col = lax.broadcasted_iota(jnp.int32, (1, lines * ROWS), 1) % ROWS
        pick = jnp.where(col % 4 >= 2, key8[1], key8[0]).astype(jnp.int32) * 8 + col
        rid = lax.broadcasted_iota(jnp.int32, (groups * slots, lines * ROWS), 0)
        inner = rid % slots
        r4 = (
            (inner >= CAP).astype(jnp.int32)
            + (inner >= 2 * CAP).astype(jnp.int32)
            + (inner >= 3 * CAP).astype(jnp.int32)
            + (inner >= 4 * CAP).astype(jnp.int32)
        )
        want = ((rid // slots) * 8 + (inner - CAP * r4)) * 8 + 4 * core + r4
        sel[...] = (want == pick).astype(F32).astype(BF16)
        for j in range(2):
            wkey[8 * j : 8 * j + 8, :] = jnp.broadcast_to(dot(keys[j], wide16), (8, lines * BINS))

        loads[2].wait()
        loads[3].wait()
        loads[1].wait()
        loads[7].wait()
        bid = lax.broadcasted_iota(jnp.int32, (BINS, 16), 0)

        def rotate(s):
            hot = (bid == binb[s]).astype(F32).astype(BF16)

            def chunk(i, carry):
                at_ = pl.ds(pl.multiple_of(i * width, LINE), width)
                ctf = dot(hot, tabh[:, at_], TN)
                for part in range(2):
                    x = ctf * xin[s, part, :, at_].astype(F32)
                    r0 = pl.multiple_of(512 + part * 32 + s * 16, 16)
                    rbuf[pl.ds(r0, 16), at_] = x.astype(BF16)
                    for u in range(8):
                        r0 = pl.multiple_of(part * 256 + u * 32 + s * 16, 16)
                        rbuf[pl.ds(r0, 16), at_] = (x * trigv[u : u + 1, at_]).astype(BF16)
                return carry

            lax.fori_loop(0, COLOURS, chunk, 0)

        rotate(core)
        for i in (0, 4, 5, 6):
            loads[i].wait()

        pl.semaphore_wait(barrier, 5 + groups - 1)

        swaps = []
        for i, (src, dst) in enumerate(
            (
                (proj.at[:, :, theirs], pin.at[core]),
                (parts.at[:, :, theirs], xin.at[core]),
                (cand, candb.at[core]),
                (bins, binb.at[core]),
            )
        ):
            swaps.append(
                pltpu.make_async_remote_copy(
                    src_ref=src, dst_ref=dst,
                    send_sem=ex_s.at[i], recv_sem=ex_r.at[i], device_id=mate, device_id_type=MESH,
                )
            )
        for c in swaps:
            c.start()
        swaps[0].wait_recv()
        for s in range(2):
            for j in range(2):
                asm[4 * s + 2 * j : 4 * s + 2 * j + 2, :] = pin[s, j].astype(F32)
        pbuf[node] = asm[...].astype(BF16)

        def span(q):
            return slice(q * width, (q + 1) * width)

        def ag(q, e, p):
            to = e | 1 << p
            m = at(offset_of(q, e))
            return pltpu.make_async_remote_copy(
                src_ref=pbuf.at[m, :, span(q)], dst_ref=pbuf.at[m, :, span(q)],
                send_sem=ag_s.at[q, to], recv_sem=ag_r.at[q, to],
                device_id=dev(STEPS[(p + q) % 4]), device_id_type=MESH,
            )

        def ag_in(q, e):
            m = at(offset_of(q, e))
            return pltpu.make_async_remote_copy(
                src_ref=pbuf.at[m, :, span(q)], dst_ref=pbuf.at[m, :, span(q)],
                send_sem=ag_s.at[q, e], recv_sem=ag_r.at[q, e],
                device_id=dev(STEPS[(top(e) + q) % 4]), device_id_type=MESH,
            )

        sent = []

        def push(c):
            c.start()
            sent.append(c)

        for p in range(4):
            for q in range(COLOURS):
                push(ag(q, 0, p))
        for e in (1,):
            for q in range(COLOURS):
                ag_in(q, e).wait_recv()
                for p in range(1, 4):
                    push(ag(q, e, p))
        for e in (2, 3):
            for q in range(COLOURS):
                ag_in(q, e).wait_recv()
                for p in range(2, 4):
                    push(ag(q, e, p))
        for e in (4, 5, 6, 7):
            for q in range(COLOURS):
                ag_in(q, e).wait_recv()
                push(ag(q, e, 3))

        swaps[1].wait_recv()
        swaps[2].wait_recv()
        swaps[3].wait_recv()
        rotate(other)

        ohb = jnp.zeros((128, 128), F32)
        cid = lax.broadcasted_iota(jnp.int32, (128, 128), 0)
        lane_core = (lanes % 32) // 16
        til = (
            lax.broadcasted_iota(jnp.int32, (16, 128), 1) % 16
            == lax.broadcasted_iota(jnp.int32, (16, 128), 0)
        ).astype(F32)
        bl = [dot(binb[s].astype(F32), til) for s in range(2)]
        blane = jnp.where(lane_core == 1, bl[1], bl[0]).astype(jnp.int32)
        ohb = (cid == blane).astype(F32)
        cl = [dot(candb[s].astype(F32), til, TN) for s in range(2)]
        clane = jnp.where(lane_core == 1, cl[1], cl[0]).astype(jnp.int32)
        jid = lax.broadcasted_iota(jnp.int32, (64, 128), 0)
        listed = jid == clane[0:1, :]
        for k in range(1, 8):
            listed = jnp.logical_or(listed, jid == clane[k : k + 1, :])

        def squares(i, carry):
            v = tabf[:, pl.ds(pl.multiple_of(i * LINE, LINE), LINE)].astype(F32)
            w3[pl.ds(pl.multiple_of(i * BINS, BINS), BINS), :] = v * v
            return carry

        lax.fori_loop(0, lines, squares, 0)
        bpscr[...] = jnp.zeros(bpscr.shape, F32)
        gscr[...] = jnp.zeros(gscr.shape, F32)

        for q in range(COLOURS):
            for e in range(8, 16):
                ag_in(q, e).wait_recv()
            p32 = pbuf[:, :, span(q)].astype(F32).reshape(NODES * ROWS, width)
            nz = noisev[:, span(q)]
            got = dot((p32 * nz).astype(BF16), rbuf[:, span(q)], NT)
            t32 = tabh[:, span(q)].astype(F32)
            ns = t32 * t32 * nz
            ns_hi = ns.astype(BF16)
            ns_lo = (ns - ns_hi.astype(F32)).astype(BF16)
            pp = p32 * p32
            pp_hi = pp.astype(BF16)
            pp_lo = (pp - pp_hi.astype(F32)).astype(BF16)
            power = dot(pp_hi, ns_hi, NT) + dot(pp_hi, ns_lo, NT) + dot(pp_lo, ns_hi, NT)
            bpscr[:, 0:BINS] += power
            for k in range(5):
                w = min(128, 576 - 128 * k)
                gscr[k, :, 0:w] += got[:, 128 * k : 128 * k + w]
        even, odd = pl.ds(0, 64, stride=2), pl.ds(1, 64, stride=2)
        ge = [gscr[k, even, :] for k in range(5)]
        go = [gscr[k, odd, :] for k in range(5)]
        sx[core, 0] = ge[0] + go[2]
        sx[core, 1] = go[1] - ge[3]
        sx[core, 2] = ge[4] + pltpu.roll(go[4], 96, 1)
        sx[core, 3] = bpscr[even, :] + bpscr[odd, :]
        trade = pltpu.make_async_remote_copy(
            src_ref=sx.at[core], dst_ref=sx.at[core], send_sem=sx_sem.at[0], recv_sem=sx_sem.at[1],
            device_id=mate, device_id_type=MESH,
        )
        trade.start()
        trade.wait_recv()

        quad = 0.5 * dot(sx[0, 3] + sx[1, 3], ohb, NN, HIGH)
        base = sx[0, 0] + sx[1, 0] - quad
        turn = sx[0, 1] + sx[1, 1]
        first = jnp.logical_and(listed, lanes < 32)
        s_plus = jnp.where(listed, base - turn, NEG)
        s_minus = jnp.where(listed, base + turn, NEG)
        s_zero = jnp.where(first, sx[0, 2] + sx[1, 2] - quad, NEG)
        peak = jnp.max(jnp.maximum(jnp.maximum(s_plus, s_minus), s_zero), axis=0, keepdims=True)
        peak = jnp.maximum(peak, pltpu.roll(peak, 32, 1))
        peak = jnp.maximum(peak, pltpu.roll(peak, 64, 1))
        e_plus = jnp.where(listed, jnp.exp(s_plus - peak), 0.0)
        e_minus = jnp.where(listed, jnp.exp(s_minus - peak), 0.0)
        e_zero = jnp.where(first, jnp.exp(s_zero - peak), 0.0)
        total = jnp.sum(e_plus + e_minus + e_zero, axis=0, keepdims=True)
        total = total + pltpu.roll(total, 32, 1)
        total = total + pltpu.roll(total, 64, 1)
        inv = 1.0 / total
        both = (e_plus + e_minus) * inv
        gap = (e_plus - e_minus) * inv
        zero = e_zero * inv
        blank = jnp.zeros((64, 128), F32)
        for k, (a, b) in enumerate(
            ((both, blank), (blank, -gap), (blank, both), (gap, blank), (zero, pltpu.roll(zero, 32, 1)))
        ):
            cscr[k, even, :] = a
            cscr[k, odd, :] = b
        share = dot(both + zero, ohb, NT, HIGH)
        bsscr[even, :] = share
        bsscr[odd, :] = blank
        coef = jnp.concatenate([cscr[k] for k in range(5)], axis=1)[:, 0:576].astype(BF16)
        dbuf[:, :, half : half + 128] = bsscr[...].reshape(NODES, ROWS, 128).astype(BF16)

        def rspan(q):
            return slice(q * width, (q + 1) * width + (128 if q == COLOURS - 1 else 0))

        def rs(q, e):
            m = at(offset_of(q, e))
            return pltpu.make_async_remote_copy(
                src_ref=dbuf.at[m, :, rspan(q)], dst_ref=rsb.at[e, :, rspan(q)],
                send_sem=rs_s.at[q, e], recv_sem=rs_r.at[q, e],
                device_id=dev(STEPS[(top(e) + q) % 4]), device_id_type=MESH,
            )

        def collect(q, e):
            m = at(offset_of(q, e))
            acc = dbuf[m, :, rspan(q)].astype(F32)
            for r in range(3, top(e) if e else -1, -1):
                child = e | 1 << r
                rs(q, child).wait_recv()
                acc = acc + rsb[child, :, rspan(q)].astype(F32)
            return m, acc

        for q in range(COLOURS):
            out = dot(coef, rbuf[:, span(q)])
            dbuf[:, :, span(q)] = out.reshape(NODES, ROWS, width).astype(BF16)
            for e in range(15, 7, -1):
                push(rs(q, e))
        for e in range(7, 0, -1):
            for q in range(COLOURS):
                m, acc = collect(q, e)
                dbuf[m, :, rspan(q)] = acc.astype(BF16)
                push(rs(q, e))
        extra = None
        for q in range(COLOURS):
            _, acc = collect(q, 0)
            zb[core, :, span(q)] = acc[:, :width].astype(BF16)
            if q == COLOURS - 1:
                extra = acc[:, width:]
        zx = pltpu.make_async_remote_copy(
            src_ref=zb.at[core], dst_ref=zb.at[core], send_sem=zx_sem.at[0], recv_sem=zx_sem.at[1],
            device_id=mate, device_id_type=MESH,
        )
        zx.start()

        rows8 = lax.broadcasted_iota(jnp.int32, (8, 128), 0)
        for j in range(2):
            wzs[j : j + 1, :] = jnp.sum(
                jnp.where(rows8 == 4 * core + 2 * j, extra, 0.0), axis=0, keepdims=True
            )
        order = sorted(range(1, groups), key=lambda k: -min(k, groups - k))

        def wmsg(k):
            return pltpu.make_async_remote_copy(
                src_ref=wzs, dst_ref=wzr.at[k], send_sem=w_s.at[k], recv_sem=w_r.at[k],
                device_id=((z + k) % groups, d), device_id_type=MESH,
            )

        def zmsg(k):
            return pltpu.make_async_remote_copy(
                src_ref=zsend.at[(z + k) % groups, 0 : 4 * CAP], dst_ref=zrecv.at[k, 0 : 4 * CAP],
                send_sem=z_s.at[k], recv_sem=z_r.at[k],
                device_id=((z + k) % groups, d), device_id_type=MESH,
            )

        for k in order:
            push(wmsg(k))
        zx.wait_recv()
        stack = jnp.concatenate(
            [
                zb[h, :, LINE * i : LINE * i + LINE].astype(F32)
                for h in range(2)
                for i in range(hl)
            ],
            axis=0,
        ).astype(BF16)
        packed = dot(sel[...], stack)
        zsend[...] = packed.astype(BF16).reshape(groups, slots, LINE)
        for k in order:
            push(zmsg(k))
        acc_w = wzs[...]
        for k in range(1, groups):
            wmsg(k).wait_recv()
            acc_w = acc_w + wzr[k]
        spread = (
            lax.broadcasted_iota(jnp.int32, (128, lines * BINS), 1) % BINS
            == lax.broadcasted_iota(jnp.int32, (128, lines * BINS), 0)
        ).astype(F32)
        scale = 64.0 / (16 * groups * NODES * 2)
        tall = jnp.concatenate(
            [jnp.broadcast_to(acc_w[j : j + 1, :] * scale, (8, 128)) for j in range(2)], axis=0
        )
        coefw = dot(tall, spread, NN, HIGH)
        slot = lax.broadcasted_iota(jnp.int32, (16, lines * BINS), 0) % 8
        ok = wkey[...].astype(jnp.int32) == z * 8 + slot
        weights = dot(jnp.where(ok, coefw, 0.0), w3[...], NN, HIGH)
        for j in range(2):
            o_weight[j] = weights[8 * j : 8 * j + CAP, :]
        acc = zsend[z, 0 : 4 * CAP].astype(F32)
        for k in range(1, groups):
            zmsg(k).wait_recv()
            acc = acc + zrecv[k, 0 : 4 * CAP].astype(F32)
        for r in range(4):
            o_data[r] = acc[CAP * r : CAP * r + CAP, :]

        for c in sent:
            c.wait_send()
        for c in swaps:
            c.wait_send()
        trade.wait_send()
        zx.wait_send()

    return kernel


def body(particles, defocus_bin, candidates, projections, ctf_table, inv_noise, line_slab, slab_owner):
    groups = lax.axis_size("grp")
    pixels = particles.shape[2]
    lines = pixels // LINE
    half = pixels // 2
    trig = jnp.asarray(phase_rows(lines))
    hbm = pl.BlockSpec(memory_space=pl.ANY)
    vmem = pl.BlockSpec(memory_space=pltpu.VMEM)
    smem = pl.BlockSpec(memory_space=pltpu.SMEM)
    dma = pltpu.SemaphoreType.DMA
    data, weight = pl.pallas_call(
        make_kernel(lines, groups),
        name="estep",
        out_shape=(
            jax.ShapeDtypeStruct((4, CAP, LINE), F32),
            jax.ShapeDtypeStruct((2, CAP, LINE), F32),
        ),
        in_specs=[hbm, hbm, hbm, hbm, hbm, vmem, vmem, vmem, smem],
        out_specs=(vmem, vmem),
        scratch_shapes=[
            pltpu.VMEM((2, 2, 16, half), BF16),
            pltpu.VMEM((2, 2, 2, half), BF16),
            pltpu.VMEM((2, 16, 8), jnp.int32),
            pltpu.VMEM((2, 1, 16), jnp.int32),
            pltpu.VMEM((8, half), F32),
            pltpu.VMEM((BINS, half), BF16),
            pltpu.VMEM((BINS, pixels), BF16),
            pltpu.VMEM((1, half), F32),
            pltpu.VMEM((8, half), F32),
            pltpu.VMEM((NODES, ROWS, half), BF16),
            pltpu.VMEM((576, half), BF16),
            pltpu.VMEM((5, 128, 128), F32),
            pltpu.VMEM((128, 128), F32),
            pltpu.VMEM((2, 4, 64, 128), F32),
            pltpu.VMEM((5, 128, 128), F32),
            pltpu.VMEM((128, 128), F32),
            pltpu.VMEM((NODES, ROWS, half + 128), BF16),
            pltpu.VMEM((NODES, ROWS, half + 128), BF16),
            pltpu.VMEM((2, ROWS, half), BF16),
            pltpu.VMEM((groups * 32, lines * ROWS), BF16),
            pltpu.VMEM((16, lines * BINS), F32),
            pltpu.VMEM((lines * BINS, LINE), F32),
            pltpu.VMEM((groups, 32, LINE), BF16),
            pltpu.VMEM((groups, 32, LINE), BF16),
            pltpu.VMEM((2, 128), F32),
            pltpu.VMEM((groups, 2, 128), F32),
            dma((8,)), dma((4,)), dma((4,)),
            dma((4, 16)), dma((4, 16)), dma((4, 16)), dma((4, 16)),
            dma((2,)), dma((2,)),
            dma((groups,)), dma((groups,)), dma((groups,)), dma((groups,)),
        ],
        compiler_params=pltpu.CompilerParams(
            collective_id=0, has_side_effects=True, vmem_limit_bytes=48 << 20
        ),
    )(
        jnp.transpose(particles, (1, 0, 2)),
        projections,
        ctf_table,
        inv_noise.reshape(1, pixels),
        trig,
        candidates,
        defocus_bin.reshape(1, 16),
        line_slab,
        slab_owner,
    )
    return (data.reshape(1, 2, 2, CAP, LINE), weight[None])


def solution(mesh):
    return jax.shard_map(
        body,
        mesh=mesh,
        in_specs=(
            P(("grp", "dev"), None, None),
            P(("grp", "dev")),
            P(("grp", "dev"), None),
            P("dev", None, None),
            P(),
            P(),
            P("dev", None),
            P(),
        ),
        out_specs=(P("grp", "dev", None, None, None), P("grp", "dev", None, None)),
        check_vma=False,
    )
```

```python
import math

import jax
import jax.numpy as jnp
import numpy as np
from jax import lax
from jax.experimental import pallas as pl
from jax.experimental.pallas import tpu as pltpu
from jax.sharding import PartitionSpec as P

LINE = 128
CAP = 6
BINS = 16
NODES = 16
COLOURS = 4
ROWS = 8
NEG = -3.0e38
MESH = pl.DeviceIdType.MESH
F32 = jnp.float32
BF16 = jnp.bfloat16
HIGH = lax.Precision.HIGHEST
NN = (((1,), (0,)), ((), ()))
NT = (((1,), (1,)), ((), ()))
TN = (((0,), (0,)), ((), ()))
STAGES = (
    ((1, 4, 5), (3, 12, 15)),
    ((3, 12, 15), (1, 4, 5)),
    ((1, 12, 13), (3, 4, 7)),
    ((3, 4, 7), (1, 12, 13)),
)
NEAR = (1, 3, 4, 12, 5, 15, 13, 7)


def dot(a, b, dims=NN, precision=None):
    return lax.dot_general(a, b, dims, preferred_element_type=F32, precision=precision)


def phase_rows(lines):
    line = np.repeat(np.arange(lines), LINE).astype(np.float64)
    column = np.tile(np.arange(LINE), lines)
    freq = np.where(column < LINE // 2, column, column - LINE).astype(np.float64)
    moves = ((0, 1), (1, -1), (1, 0), (1, 1))
    angle = np.stack([dx * line + dy * freq for dx, dy in moves]) * (2.0 * math.pi / LINE)
    return np.concatenate([np.cos(angle), np.sin(angle)]).astype(np.float32)


def flip(v, k):
    if k == 0:
        return v
    if k == 1:
        return v + 1 - 2 * (v % 2)
    if k == 2:
        return (v + 2) % 4
    return 3 - v


def make_kernel(lines, groups):
    half = lines * LINE // 2
    width = half // COLOURS
    hl = lines // 2
    slots = 32

    def kernel(parts, proj, table, noise, trig, cand, bins, slab, owner,
               o_data, o_weight,
               xin, xs, ctfv, candb, binb, slabv, owners, trigv, tabh, tabf, noisev, pbuf, ps, rbuf,
               gscr, bpscr, sx, cscr, bsscr, dbuf, rsb, zb, sel, wkey, w3, zsend, zrecv, wzs, wzr,
               loc, ex_s, ex_r, ag_s, ag_r, rs_s, rs_r, sx_sem, zx_sem, z_s, z_r, w_s, w_r, ring):
        z = lax.axis_index("grp")
        d = lax.axis_index("dev")
        core = d % 2
        node = d // 2
        nx, ny = node % 4, node // 4
        other = 1 - core

        def dev(k, c):
            return (z, (flip(ny, k // 4) * 4 + flip(nx, k % 4)) * 2 + c)

        def along(k):
            return ((z + k + groups) % groups, d)

        mate = (z, node * 2 + other)

        def greet(sem, to):
            pl.semaphore_signal(sem, inc=1, device_id=to, device_id_type=MESH)

        barrier = pltpu.get_barrier_semaphore()
        greet(barrier, mate)
        for k in NEAR:
            greet(barrier, dev(k, core))
            greet(barrier, dev(k, other))
        greet(barrier, along(1))
        greet(barrier, along(-1))

        mine = pl.multiple_of(core * half, LINE)
        theirs = pl.multiple_of(other * half, LINE)
        loads = [
            pltpu.make_async_copy(bins, binb.at[core], loc.at[0]),
            pltpu.make_async_copy(table.at[:, pl.ds(mine, half)], tabh, loc.at[1]),
            pltpu.make_async_copy(parts.at[:, :, pl.ds(mine, half)], xin.at[core], loc.at[2]),
            pltpu.make_async_copy(trig.at[:, pl.ds(mine, half)], trigv, loc.at[3]),
            pltpu.make_async_copy(proj.at[:, :, pl.ds(mine, half)], pbuf.at[0, core], loc.at[4]),
            pltpu.make_async_copy(noise.at[:, pl.ds(mine, half)], noisev, loc.at[5]),
            pltpu.make_async_copy(cand, candb.at[core], loc.at[6]),
            pltpu.make_async_copy(slab, slabv, loc.at[7]),
            pltpu.make_async_copy(table, tabf, loc.at[8]),
            pltpu.make_async_copy(owner, owners, loc.at[9]),
        ]
        for c in loads:
            c.start()

        pl.semaphore_wait(barrier, 3 + 2 * len(NEAR))

        def span(q):
            return slice(q * width, (q + 1) * width)

        def cast(q, t, c):
            side = pl.multiple_of((mine if c is core else theirs) + q * width, LINE)
            return pltpu.make_async_remote_copy(
                src_ref=proj.at[:, :, pl.ds(side, width)],
                dst_ref=pbuf.at[t, core, :, :, span(q)],
                send_sem=ag_s.at[q, t, 0 if c is core else 1], recv_sem=ag_r.at[q, t, core],
                device_id=dev(t, c), device_id_type=MESH,
            )

        def relay(q, k, s, t):
            return pltpu.make_async_remote_copy(
                src_ref=pbuf.at[k, s, :, :, span(q)], dst_ref=pbuf.at[k ^ t, s, :, :, span(q)],
                send_sem=ag_s.at[q, k ^ t, s], recv_sem=ag_r.at[q, k ^ t, s],
                device_id=dev(t, core), device_id_type=MESH,
            )

        def arrived(q, k, s):
            pltpu.make_async_remote_copy(
                src_ref=pbuf.at[k, s, :, :, span(q)], dst_ref=pbuf.at[k, s, :, :, span(q)],
                send_sem=ag_s.at[q, k, s], recv_sem=ag_r.at[q, k, s],
                device_id=dev(k, core), device_id_type=MESH,
            ).wait_recv()

        sent = []

        def push(c):
            c.start()
            sent.append(c)

        for stage in range(2):
            for i in (2, 0, 1):
                for q in range(COLOURS):
                    push(cast(q, STAGES[q][stage][i], core))
                    push(cast(q, STAGES[q][stage][i], other))
        swaps = [
            pltpu.make_async_remote_copy(
                src_ref=src, dst_ref=dst, send_sem=ex_s.at[i], recv_sem=ex_r.at[i],
                device_id=mate, device_id_type=MESH,
            )
            for i, (src, dst) in enumerate(
                (
                    (proj.at[:, :, pl.ds(theirs, half)], pbuf.at[0, core]),
                    (bins, binb.at[core]),
                    (cand, candb.at[core]),
                    (parts.at[:, :, pl.ds(theirs, half)], xin.at[core]),
                )
            )
        ]
        for c in swaps:
            push(c)
        reach = 1
        rounds = []
        while 2 * reach <= groups // 2:
            rounds.append(reach)
            reach *= 2
        if rounds:
            greet(ring.at[0], along(1))
            greet(ring.at[0], along(-1))

        def spread_word(i):
            if i < len(rounds):
                pl.semaphore_wait(ring.at[i], 2)
                if i + 1 < len(rounds):
                    greet(ring.at[i + 1], along(rounds[i + 1]))
                    greet(ring.at[i + 1], along(-rounds[i + 1]))

        even2, odd2 = pl.ds(0, 16, stride=2), pl.ds(1, 16, stride=2)
        bid = lax.broadcasted_iota(jnp.int32, (BINS, 16), 0)

        def rotate(s):
            hot = (bid == binb[s]).astype(F32).astype(BF16)
            ctfv[...] = dot(hot, tabh[...], TN)

            def chunk(i, carry):
                for t in range(width // LINE):
                    at_ = pl.ds(pl.multiple_of(i * width + t * LINE, LINE), LINE)
                    for p in range(16):
                        xs[t, 2 * p : 2 * p + 2, :] = xin[s, p, :, at_].astype(F32)
                    for part in range(2):
                        x = ctfv[:, at_] * xs[t, even2 if part == 0 else odd2, :]
                        r0 = pl.multiple_of(512 + part * 32 + s * 16, 16)
                        rbuf[pl.ds(r0, 16), at_] = x.astype(BF16)
                        for u in range(8):
                            r0 = pl.multiple_of(part * 256 + u * 32 + s * 16, 16)
                            rbuf[pl.ds(r0, 16), at_] = (x * trigv[u : u + 1, at_]).astype(BF16)
                return carry

            lax.fori_loop(0, COLOURS, chunk, 0)

        for i in range(4):
            loads[i].wait()
        rotate(core)
        for i in range(3):
            for q in range(COLOURS):
                k = STAGES[q][0][i]
                for s in range(2):
                    arrived(q, k, s)
                    for t in STAGES[q][1][::-1]:
                        push(relay(q, k, s, t))
        spread_word(0)
        swaps[1].wait_recv()
        swaps[3].wait_recv()
        rotate(other)

        for i in range(4, 10):
            loads[i].wait()
        swaps[2].wait_recv()
        lanes = lax.broadcasted_iota(jnp.int32, (1, 128), 1)
        cid = lax.broadcasted_iota(jnp.int32, (128, 128), 0)
        lane_core = (lanes % 32) // 16
        til = (
            lax.broadcasted_iota(jnp.int32, (16, 128), 1) % 16
            == lax.broadcasted_iota(jnp.int32, (16, 128), 0)
        ).astype(F32)
        bl = [dot(binb[s].astype(F32), til) for s in range(2)]
        blane = jnp.where(lane_core == 1, bl[1], bl[0]).astype(jnp.int32)
        ohb = (cid == blane).astype(F32)
        cl = [dot(candb[s].astype(F32), til) for s in range(2)]
        clane = jnp.where(lane_core == 1, cl[1], cl[0]).astype(jnp.int32)
        rid = lax.broadcasted_iota(jnp.int32, (64, 128), 0)
        jid = ((rid // 4) ^ node) * 4 + rid % 4
        listed = jid == clane[0:1, :]
        for k in range(1, 8):
            listed = jnp.logical_or(listed, jid == clane[k : k + 1, :])
        bpscr[...] = jnp.zeros(bpscr.shape, F32)
        gscr[...] = jnp.zeros(gscr.shape, F32)
        spread_word(1)

        def score(q, ks):
            for i, k in enumerate(ks):
                for s in range(2):
                    for j in range(2):
                        r = 8 * i + 4 * s + 2 * j
                        ps[r : r + 2, :] = pbuf[k, s, j, :, span(q)].astype(F32)
            p32 = ps[0 : 8 * len(ks), :]
            nz = noisev[:, span(q)]
            got = dot((p32 * nz).astype(BF16), rbuf[:, span(q)], NT)
            t32 = tabh[:, span(q)].astype(F32)
            ns = t32 * t32 * nz
            ns_hi = ns.astype(BF16)
            ns_lo = (ns - ns_hi.astype(F32)).astype(BF16)
            pp = p32 * p32
            pp_hi = pp.astype(BF16)
            pp_lo = (pp - pp_hi.astype(F32)).astype(BF16)
            power = dot(pp_hi, ns_hi, NT) + dot(pp_hi, ns_lo, NT) + dot(pp_lo, ns_hi, NT)
            for i, k in enumerate(ks):
                here, there = slice(8 * i, 8 * i + 8), slice(8 * k, 8 * k + 8)
                bpscr[there, 0:BINS] += power[here, :]
                for b in range(5):
                    w = min(128, 576 - 128 * b)
                    gscr[b, there, 0:w] += got[here, 128 * b : 128 * b + w]

        swaps[0].wait_recv()
        for q in range(COLOURS):
            for k in STAGES[q][1]:
                for s in range(2):
                    arrived(q, k, s)
            score(q, (0,) + STAGES[q][0] + STAGES[q][1])
        for q in range(COLOURS):
            late = tuple(a ^ b for a in STAGES[q][0] for b in STAGES[q][1])
            for k in late:
                for s in range(2):
                    arrived(q, k, s)
            score(q, late)
        even, odd = pl.ds(0, 64, stride=2), pl.ds(1, 64, stride=2)
        ge = [gscr[k, even, :] for k in range(5)]
        go = [gscr[k, odd, :] for k in range(5)]
        sx[core, 0] = ge[0] + go[2]
        sx[core, 1] = go[1] - ge[3]
        sx[core, 2] = jnp.where(
            lanes < 32, ge[4] + pltpu.roll(go[4], 96, 1), pltpu.roll(bpscr[even, :] + bpscr[odd, :], 64, 1)
        )
        trade = pltpu.make_async_remote_copy(
            src_ref=sx.at[core], dst_ref=sx.at[core], send_sem=sx_sem.at[0], recv_sem=sx_sem.at[1],
            device_id=mate, device_id_type=MESH,
        )
        push(trade)
        trade.wait_recv()

        last = sx[0, 2] + sx[1, 2]
        power = jnp.where(lanes < BINS, pltpu.roll(last, 64, 1), 0.0)
        quad = 0.5 * dot(power, ohb, NN, HIGH)
        base = sx[0, 0] + sx[1, 0] - quad
        turn = sx[0, 1] + sx[1, 1]
        first = jnp.logical_and(listed, lanes < 32)
        s_plus = jnp.where(listed, base - turn, NEG)
        s_minus = jnp.where(listed, base + turn, NEG)
        s_zero = jnp.where(first, last - quad, NEG)
        peak = jnp.max(jnp.maximum(jnp.maximum(s_plus, s_minus), s_zero), axis=0, keepdims=True)
        peak = jnp.maximum(peak, pltpu.roll(peak, 32, 1))
        peak = jnp.maximum(peak, pltpu.roll(peak, 64, 1))
        e_plus = jnp.where(listed, jnp.exp(s_plus - peak), 0.0)
        e_minus = jnp.where(listed, jnp.exp(s_minus - peak), 0.0)
        e_zero = jnp.where(first, jnp.exp(s_zero - peak), 0.0)
        total = jnp.sum(e_plus + e_minus + e_zero, axis=0, keepdims=True)
        total = total + pltpu.roll(total, 32, 1)
        total = total + pltpu.roll(total, 64, 1)
        inv = 1.0 / total
        both = (e_plus + e_minus) * inv
        gap = (e_plus - e_minus) * inv
        zero = e_zero * inv
        blank = jnp.zeros((64, 128), F32)
        for k, (a, b) in enumerate(
            ((both, blank), (blank, -gap), (blank, both), (gap, blank), (zero, pltpu.roll(zero, 32, 1)))
        ):
            cscr[k, even, :] = a
            cscr[k, odd, :] = b
        share = dot(both + zero, ohb, NT, HIGH)
        bsscr[even, :] = share
        bsscr[odd, :] = blank
        coef = jnp.concatenate([cscr[k] for k in range(5)], axis=1)[:, 0:576].astype(BF16)
        dbuf[:, :, half : half + 128] = bsscr[...].reshape(NODES, ROWS, 128).astype(BF16)

        def rspan(q):
            return slice(q * width, (q + 1) * width + (128 if q == COLOURS - 1 else 0))

        def rs(q, k, t):
            return pltpu.make_async_remote_copy(
                src_ref=dbuf.at[k, :, rspan(q)], dst_ref=rsb.at[k, :, rspan(q)],
                send_sem=rs_s.at[q, k], recv_sem=rs_r.at[q, k],
                device_id=dev(t, core), device_id_type=MESH,
            )

        def collect(q, k, froms):
            acc = dbuf[k, :, rspan(q)].astype(F32)
            for child in froms:
                rs(q, child, child ^ k).wait_recv()
                acc = acc + rsb[child, :, rspan(q)].astype(F32)
            return acc

        for q in range(COLOURS):
            out = dot(coef, rbuf[:, span(q)])
            dbuf[:, :, span(q)] = out.reshape(NODES, ROWS, width).astype(BF16)
            for k in STAGES[q][0] + (0,):
                for t in STAGES[q][1][::-1]:
                    push(rs(q, k ^ t, t))

        lid = lax.broadcasted_iota(jnp.int32, (groups, lines), 0)
        tri = (
            lax.broadcasted_iota(jnp.int32, (lines, lines), 0)
            < lax.broadcasted_iota(jnp.int32, (lines, lines), 1)
        ).astype(F32)
        wide = (
            lax.broadcasted_iota(jnp.int32, (lines, lines * ROWS), 1) // ROWS
            == lax.broadcasted_iota(jnp.int32, (lines, lines * ROWS), 0)
        ).astype(F32)
        wide16 = (
            lax.broadcasted_iota(jnp.int32, (lines, lines * BINS), 1) // BINS
            == lax.broadcasted_iota(jnp.int32, (lines, lines * BINS), 0)
        ).astype(F32)
        keys = []
        for j in range(2):
            row = slabv[j : j + 1, :]
            own = jnp.zeros((1, lines), jnp.int32)
            for s in range(groups):
                own = own + jnp.where(row == s, owners[0, s], 0)
            hit = (lid == own).astype(F32)
            rank = jnp.sum(hit * dot(hit, tri), axis=0, keepdims=True)
            keys.append((own * 8).astype(F32) + rank)
        key8 = [dot(k, wide) for k in keys]
        col = lax.broadcasted_iota(jnp.int32, (1, lines * ROWS), 1) % ROWS
        pick = jnp.where(col % 4 >= 2, key8[1], key8[0]).astype(jnp.int32) * 8 + col
        rid = lax.broadcasted_iota(jnp.int32, (groups * slots, lines * ROWS), 0)
        inner = rid % slots
        r4 = (
            (inner >= CAP).astype(jnp.int32)
            + (inner >= 2 * CAP).astype(jnp.int32)
            + (inner >= 3 * CAP).astype(jnp.int32)
            + (inner >= 4 * CAP).astype(jnp.int32)
        )
        want = ((rid // slots) * 8 + (inner - CAP * r4)) * 8 + 4 * core + r4
        sel[...] = (want == pick).astype(F32).astype(BF16)
        for j in range(2):
            wkey[8 * j : 8 * j + 8, :] = jnp.broadcast_to(dot(keys[j], wide16), (8, lines * BINS))

        for i in range(3):
            for q in range(COLOURS):
                k = STAGES[q][0][i]
                acc = collect(q, k, [k ^ t for t in STAGES[q][1]])
                dbuf[k, :, rspan(q)] = acc.astype(BF16)
                push(rs(q, k, k))

        def squares(i, carry):
            v = tabf[:, pl.ds(pl.multiple_of(i * LINE, LINE), LINE)].astype(F32)
            w3[pl.ds(pl.multiple_of(i * BINS, BINS), BINS), :] = v * v
            return carry

        lax.fori_loop(0, lines, squares, 0)
        spread_word(2)
        extra = None
        for q in range(COLOURS):
            acc = collect(q, 0, STAGES[q][1] + STAGES[q][0])
            zb[core, :, span(q)] = acc[:, :width].astype(BF16)
            if q == COLOURS - 1:
                extra = acc[:, width:]
        zx = pltpu.make_async_remote_copy(
            src_ref=zb.at[core], dst_ref=zb.at[core], send_sem=zx_sem.at[0], recv_sem=zx_sem.at[1],
            device_id=mate, device_id_type=MESH,
        )
        push(zx)

        rows8 = lax.broadcasted_iota(jnp.int32, (8, 128), 0)
        for j in range(2):
            wzs[j : j + 1, :] = jnp.sum(
                jnp.where(rows8 == 4 * core + 2 * j, extra, 0.0), axis=0, keepdims=True
            )
        order = sorted(range(1, groups), key=lambda k: -min(k, groups - k))

        def wmsg(k):
            return pltpu.make_async_remote_copy(
                src_ref=wzs, dst_ref=wzr.at[k], send_sem=w_s.at[k], recv_sem=w_r.at[k],
                device_id=((z + k) % groups, d), device_id_type=MESH,
            )

        def zmsg(k):
            return pltpu.make_async_remote_copy(
                src_ref=zsend.at[(z + k) % groups, 0 : 4 * CAP], dst_ref=zrecv.at[k, 0 : 4 * CAP],
                send_sem=z_s.at[k], recv_sem=z_r.at[k],
                device_id=((z + k) % groups, d), device_id_type=MESH,
            )

        for k in order:
            push(wmsg(k))
        zx.wait_recv()
        stack = jnp.concatenate(
            [
                zb[h, :, LINE * i : LINE * i + LINE].astype(F32)
                for h in range(2)
                for i in range(hl)
            ],
            axis=0,
        ).astype(BF16)
        packed = dot(sel[...], stack)
        zsend[...] = packed.astype(BF16).reshape(groups, slots, LINE)
        for k in order:
            push(zmsg(k))
        acc_w = wzs[...]
        for k in range(1, groups):
            wmsg(k).wait_recv()
            acc_w = acc_w + wzr[k]
        spread = (
            lax.broadcasted_iota(jnp.int32, (128, lines * BINS), 1) % BINS
            == lax.broadcasted_iota(jnp.int32, (128, lines * BINS), 0)
        ).astype(F32)
        scale = 64.0 / (16 * groups * NODES * 2)
        tall = jnp.concatenate(
            [jnp.broadcast_to(acc_w[j : j + 1, :] * scale, (8, 128)) for j in range(2)], axis=0
        )
        coefw = dot(tall, spread, NN, HIGH)
        slot = lax.broadcasted_iota(jnp.int32, (16, lines * BINS), 0) % 8
        ok = wkey[...].astype(jnp.int32) == z * 8 + slot
        weights = dot(jnp.where(ok, coefw, 0.0), w3[...], NN, HIGH)
        for j in range(2):
            o_weight[j] = weights[8 * j : 8 * j + CAP, :]
        acc = zsend[z, 0 : 4 * CAP].astype(F32)
        for k in range(1, groups):
            zmsg(k).wait_recv()
            acc = acc + zrecv[k, 0 : 4 * CAP].astype(F32)
        for r in range(4):
            o_data[r] = acc[CAP * r : CAP * r + CAP, :]

        for c in sent:
            c.wait_send()

    return kernel


def body(particles, defocus_bin, candidates, projections, ctf_table, inv_noise, line_slab, slab_owner):
    groups = lax.axis_size("grp")
    pixels = particles.shape[2]
    lines = pixels // LINE
    half = pixels // 2
    trig = jnp.asarray(phase_rows(lines))
    hbm = pl.BlockSpec(memory_space=pl.ANY)
    vmem = pl.BlockSpec(memory_space=pltpu.VMEM)
    dma = pltpu.SemaphoreType.DMA
    data, weight = pl.pallas_call(
        make_kernel(lines, groups),
        name="estep",
        out_shape=(
            jax.ShapeDtypeStruct((4, CAP, LINE), F32),
            jax.ShapeDtypeStruct((2, CAP, LINE), F32),
        ),
        in_specs=[hbm] * 9,
        out_specs=(vmem, vmem),
        scratch_shapes=[
            pltpu.VMEM((2, 16, 2, half), BF16),
            pltpu.VMEM((half // COLOURS // LINE, 32, LINE), F32),
            pltpu.VMEM((16, half), F32),
            pltpu.VMEM((2, 8, 16), jnp.int32),
            pltpu.VMEM((2, 1, 16), jnp.int32),
            pltpu.VMEM((2, lines), jnp.int32),
            pltpu.SMEM((1, groups), jnp.int32),
            pltpu.VMEM((8, half), F32),
            pltpu.VMEM((BINS, half), BF16),
            pltpu.VMEM((BINS, pixels), BF16),
            pltpu.VMEM((1, half), F32),
            pltpu.VMEM((NODES, 2, 2, 2, half), BF16),
            pltpu.VMEM((128, half // COLOURS), F32),
            pltpu.VMEM((576, half), BF16),
            pltpu.VMEM((5, 128, 128), F32),
            pltpu.VMEM((128, 128), F32),
            pltpu.VMEM((2, 3, 64, 128), F32),
            pltpu.VMEM((5, 128, 128), F32),
            pltpu.VMEM((128, 128), F32),
            pltpu.VMEM((NODES, ROWS, half + 128), BF16),
            pltpu.VMEM((NODES, ROWS, half + 128), BF16),
            pltpu.VMEM((2, ROWS, half), BF16),
            pltpu.VMEM((groups * 32, lines * ROWS), BF16),
            pltpu.VMEM((16, lines * BINS), F32),
            pltpu.VMEM((lines * BINS, LINE), F32),
            pltpu.VMEM((groups, 32, LINE), BF16),
            pltpu.VMEM((groups, 32, LINE), BF16),
            pltpu.VMEM((2, 128), F32),
            pltpu.VMEM((groups, 2, 128), F32),
            dma((10,)), dma((4,)), dma((4,)),
            dma((4, 16, 2)), dma((4, 16, 2)), dma((4, 16)), dma((4, 16)),
            dma((2,)), dma((2,)),
            dma((groups,)), dma((groups,)), dma((groups,)), dma((groups,)),
            pltpu.SemaphoreType.REGULAR((3,)),
        ],
        compiler_params=pltpu.CompilerParams(
            collective_id=0, has_side_effects=True, vmem_limit_bytes=67043328
        ),
    )(
        particles,
        projections,
        ctf_table,
        inv_noise.reshape(1, pixels),
        trig,
        candidates.T,
        defocus_bin.reshape(1, 16),
        line_slab,
        slab_owner.reshape(1, groups),
    )
    return (data.reshape(1, 2, 2, CAP, LINE), weight[None])


def solution(mesh):
    return jax.shard_map(
        body,
        mesh=mesh,
        in_specs=(
            P(("grp", "dev"), None, None),
            P(("grp", "dev")),
            P(("grp", "dev"), None),
            P("dev", None, None),
            P(),
            P(),
            P("dev", None),
            P(),
        ),
        out_specs=(P("grp", "dev", None, None, None), P("grp", "dev", None, None)),
        check_vma=False,
    )
```

```python
import math

import jax
import jax.numpy as jnp
import numpy as np
from jax import lax
from jax.experimental import pallas as pl
from jax.experimental.pallas import tpu as pltpu
from jax.sharding import PartitionSpec as P

LINE = 128
CAP = 6
BINS = 16
NODES = 16
COLOURS = 2
CHUNKS = 4
ROWS = 8
NEG = -3.0e38
MESH = pl.DeviceIdType.MESH
F32 = jnp.float32
BF16 = jnp.bfloat16
HIGH = lax.Precision.HIGHEST
NN = (((1,), (0,)), ((), ()))
NT = (((1,), (1,)), ((), ()))
TN = (((0,), (0,)), ((), ()))
STAGES = (
    ((1, 4, 5), (3, 12, 15)),
    ((3, 12, 15), (1, 4, 5)),
)
NEAR = (1, 3, 4, 12, 5, 15)


def dot(a, b, dims=NN, precision=None):
    return lax.dot_general(a, b, dims, preferred_element_type=F32, precision=precision)


def phase_rows(lines):
    line = np.repeat(np.arange(lines), LINE).astype(np.float64)
    column = np.tile(np.arange(LINE), lines)
    freq = np.where(column < LINE // 2, column, column - LINE).astype(np.float64)
    moves = ((0, 1), (1, -1), (1, 0), (1, 1))
    angle = np.stack([dx * line + dy * freq for dx, dy in moves]) * (2.0 * math.pi / LINE)
    return np.concatenate([np.cos(angle), np.sin(angle)]).astype(np.float32)


def flip(v, k):
    if k == 0:
        return v
    if k == 1:
        return v + 1 - 2 * (v % 2)
    if k == 2:
        return (v + 2) % 4
    return 3 - v


def make_kernel(lines, groups):
    half = lines * LINE // 2
    width = half // COLOURS
    hl = lines // 2
    piece = half // CHUNKS
    slots = 32

    def kernel(parts, proj, table, noise, trig, cand, bins, slab, owner,
               o_data, o_weight,
               xin, xs, ctfv, candb, binb, slabv, owners, trigv, tabh, tabf, noisev, nsv, pbuf, ps, rbuf,
               gscr, bpscr, sx, cscr, bsscr, dbuf, rsb, zb, sel, wkey, w3, zsend, zrecv, wzs, wzr,
               loc, ex_s, ex_r, ag_s, ag_a, ag_b, ag_l, rs_s, rs_a, rs_b, sx_sem, zx_sem, z_sem, w_sem, ring):
        z = lax.axis_index("grp")
        d = lax.axis_index("dev")
        core = d % 2
        node = d // 2
        nx, ny = node % 4, node // 4
        other = 1 - core

        def dev(k, c):
            return (z, (flip(ny, k // 4) * 4 + flip(nx, k % 4)) * 2 + c)

        def along(k):
            return ((z + k + groups) % groups, d)

        mate = (z, node * 2 + other)

        def greet(sem, to):
            pl.semaphore_signal(sem, inc=1, device_id=to, device_id_type=MESH)

        barrier = pltpu.get_barrier_semaphore()
        greet(barrier, mate)
        for k in NEAR:
            greet(barrier, dev(k, core))
            greet(barrier, dev(k, other))
        greet(barrier, along(1))
        greet(barrier, along(-1))

        mine = pl.multiple_of(core * half, LINE)
        theirs = pl.multiple_of(other * half, LINE)
        loads = [
            pltpu.make_async_copy(bins, binb.at[core], loc.at[0]),
            pltpu.make_async_copy(table.at[:, pl.ds(mine, half)], tabh, loc.at[1]),
            pltpu.make_async_copy(parts.at[:, :, pl.ds(mine, half)], xin.at[core], loc.at[2]),
            pltpu.make_async_copy(trig.at[:, pl.ds(mine, half)], trigv, loc.at[3]),
            pltpu.make_async_copy(proj.at[:, :, pl.ds(mine, half)], pbuf.at[0, core], loc.at[4]),
            pltpu.make_async_copy(noise.at[:, pl.ds(mine, half)], noisev, loc.at[5]),
            pltpu.make_async_copy(cand, candb.at[core], loc.at[6]),
            pltpu.make_async_copy(slab, slabv, loc.at[7]),
            pltpu.make_async_copy(table, tabf, loc.at[8]),
            pltpu.make_async_copy(owner, owners, loc.at[9]),
        ]
        for c in loads:
            c.start()

        pl.semaphore_wait(barrier, 3 + 2 * len(NEAR))

        def span(q):
            return slice(q * width, (q + 1) * width)

        def cast(q, t, c):
            side = pl.multiple_of((mine if c is core else theirs) + q * width, LINE)
            return pltpu.make_async_remote_copy(
                src_ref=proj.at[:, :, pl.ds(side, width)],
                dst_ref=pbuf.at[t, core, :, :, span(q)],
                send_sem=ag_s.at[0],
                recv_sem=ag_a.at[q, STAGES[q][0].index(t)] if t in STAGES[q][0] else ag_b.at[q],
                device_id=dev(t, c), device_id_type=MESH,
            )

        def relay(q, k, s, t):
            return pltpu.make_async_remote_copy(
                src_ref=pbuf.at[k, s, :, :, span(q)], dst_ref=pbuf.at[k ^ t, s, :, :, span(q)],
                send_sem=ag_s.at[0], recv_sem=ag_l.at[q],
                device_id=dev(t, core), device_id_type=MESH,
            )

        def settle(ref, send, recv):
            return pltpu.make_async_remote_copy(
                src_ref=ref, dst_ref=ref, send_sem=send, recv_sem=recv, device_id=mate, device_id_type=MESH,
            )

        sent = []

        def push(c):
            c.start()
            sent.append(c)

        for stage in range(2):
            for i in (2, 0, 1):
                for q in range(COLOURS):
                    cast(q, STAGES[q][stage][i], core).start()
                    cast(q, STAGES[q][stage][i], other).start()
        swaps = [
            pltpu.make_async_remote_copy(
                src_ref=src, dst_ref=dst, send_sem=ex_s.at[i], recv_sem=ex_r.at[i],
                device_id=mate, device_id_type=MESH,
            )
            for i, (src, dst) in enumerate(
                (
                    (proj.at[:, :, pl.ds(theirs, half)], pbuf.at[0, core]),
                    (bins, binb.at[core]),
                    (cand, candb.at[core]),
                    (parts.at[:, :, pl.ds(theirs, half)], xin.at[core]),
                )
            )
        ]
        for c in swaps:
            push(c)
        reach = 1
        rounds = []
        while 2 * reach <= groups // 2:
            rounds.append(reach)
            reach *= 2
        if rounds:
            greet(ring.at[0], along(1))
            greet(ring.at[0], along(-1))

        def spread_word(i):
            if i < len(rounds):
                pl.semaphore_wait(ring.at[i], 2)
                if i + 1 < len(rounds):
                    greet(ring.at[i + 1], along(rounds[i + 1]))
                    greet(ring.at[i + 1], along(-rounds[i + 1]))

        even2, odd2 = pl.ds(0, 16, stride=2), pl.ds(1, 16, stride=2)
        bid = lax.broadcasted_iota(jnp.int32, (BINS, 16), 0)

        def rotate(s):
            hot = (bid == binb[s]).astype(F32).astype(BF16)
            ctfv[...] = dot(hot, tabh[...], TN)

            def chunk(i, carry):
                for t in range(piece // LINE):
                    at_ = pl.ds(pl.multiple_of(i * piece + t * LINE, LINE), LINE)
                    for p in range(16):
                        xs[t, 2 * p : 2 * p + 2, :] = xin[s, p, :, at_].astype(F32)
                    for part in range(2):
                        x = ctfv[:, at_] * xs[t, even2 if part == 0 else odd2, :]
                        r0 = pl.multiple_of(512 + part * 32 + s * 16, 16)
                        rbuf[pl.ds(r0, 16), at_] = x.astype(BF16)
                        for u in range(8):
                            r0 = pl.multiple_of(part * 256 + u * 32 + s * 16, 16)
                            rbuf[pl.ds(r0, 16), at_] = (x * trigv[u : u + 1, at_]).astype(BF16)
                return carry

            lax.fori_loop(0, CHUNKS, chunk, 0)

        for i in range(4):
            loads[i].wait()
        rotate(core)
        for i in range(3):
            for q in range(COLOURS):
                k = STAGES[q][0][i]
                settle(pbuf.at[k, :, :, :, span(q)], ag_s.at[0], ag_a.at[q, i]).wait_recv()
                for t in STAGES[q][1][::-1]:
                    for s in range(2):
                        relay(q, k, s, t).start()
        spread_word(0)
        swaps[1].wait_recv()
        swaps[3].wait_recv()
        rotate(other)

        for i in range(4, 10):
            loads[i].wait()
        swaps[2].wait_recv()
        lanes = lax.broadcasted_iota(jnp.int32, (1, 128), 1)
        cid = lax.broadcasted_iota(jnp.int32, (128, 128), 0)
        lane_core = (lanes % 32) // 16
        til = (
            lax.broadcasted_iota(jnp.int32, (16, 128), 1) % 16
            == lax.broadcasted_iota(jnp.int32, (16, 128), 0)
        ).astype(F32)
        bl = [dot(binb[s].astype(F32), til) for s in range(2)]
        blane = jnp.where(lane_core == 1, bl[1], bl[0]).astype(jnp.int32)
        ohb = (cid == blane).astype(F32)
        cl = [dot(candb[s].astype(F32), til) for s in range(2)]
        clane = jnp.where(lane_core == 1, cl[1], cl[0]).astype(jnp.int32)
        rid = lax.broadcasted_iota(jnp.int32, (64, 128), 0)
        jid = ((rid // 4) ^ node) * 4 + rid % 4
        listed = jid == clane[0:1, :]
        for k in range(1, 8):
            listed = jnp.logical_or(listed, jid == clane[k : k + 1, :])
        t32 = tabh[...].astype(F32)
        ns32 = t32 * t32 * noisev[...]
        ns_hi = ns32.astype(BF16)
        nsv[0:BINS, :] = ns_hi
        nsv[BINS : 2 * BINS, :] = (ns32 - ns_hi.astype(F32)).astype(BF16)
        bpscr[...] = jnp.zeros(bpscr.shape, F32)
        gscr[...] = jnp.zeros(gscr.shape, F32)
        spread_word(1)

        def score(q, ks):
            for i, k in enumerate(ks):
                for s in range(2):
                    for j in range(2):
                        r = 8 * i + 4 * s + 2 * j
                        ps[r : r + 2, :] = pbuf[k, s, j, :, span(q)].astype(F32)
            p32 = ps[0 : 8 * len(ks), :]
            nz = noisev[:, span(q)]
            got = dot((p32 * nz).astype(BF16), rbuf[:, span(q)], NT)
            pp = p32 * p32
            pp_hi = pp.astype(BF16)
            pp_lo = (pp - pp_hi.astype(F32)).astype(BF16)
            ns = nsv[:, span(q)]
            power = dot(pp_hi, ns, NT)
            power = power[:, 0:BINS] + power[:, BINS : 2 * BINS] + dot(pp_lo, ns[0:BINS], NT)
            for i, k in enumerate(ks):
                here, there = slice(8 * i, 8 * i + 8), slice(8 * k, 8 * k + 8)
                bpscr[there, 0:BINS] += power[here, :]
                for b in range(5):
                    w = min(128, 576 - 128 * b)
                    gscr[b, there, 0:w] += got[here, 128 * b : 128 * b + w]

        swaps[0].wait_recv()
        for q in range(COLOURS):
            settle(pbuf.at[1:4, :, :, :, span(q)], ag_s.at[0], ag_b.at[q]).wait_recv()
            score(q, (0,) + STAGES[q][0] + STAGES[q][1])
        for q in range(COLOURS):
            late = tuple(a ^ b for a in STAGES[q][0] for b in STAGES[q][1])
            settle(pbuf.at[1:10, :, :, :, span(q)], ag_s.at[0], ag_l.at[q]).wait_recv()
            score(q, late)
        even, odd = pl.ds(0, 64, stride=2), pl.ds(1, 64, stride=2)
        ge = [gscr[k, even, :] for k in range(5)]
        go = [gscr[k, odd, :] for k in range(5)]
        sx[core, 0] = ge[0] + go[2]
        sx[core, 1] = go[1] - ge[3]
        sx[core, 2] = jnp.where(
            lanes < 32, ge[4] + pltpu.roll(go[4], 96, 1), pltpu.roll(bpscr[even, :] + bpscr[odd, :], 64, 1)
        )
        trade = pltpu.make_async_remote_copy(
            src_ref=sx.at[core], dst_ref=sx.at[core], send_sem=sx_sem.at[0], recv_sem=sx_sem.at[1],
            device_id=mate, device_id_type=MESH,
        )
        push(trade)
        trade.wait_recv()

        last = sx[0, 2] + sx[1, 2]
        power = jnp.where(lanes < BINS, pltpu.roll(last, 64, 1), 0.0)
        quad = 0.5 * dot(power, ohb, NN, HIGH)
        base = sx[0, 0] + sx[1, 0] - quad
        turn = sx[0, 1] + sx[1, 1]
        first = jnp.logical_and(listed, lanes < 32)
        s_plus = jnp.where(listed, base - turn, NEG)
        s_minus = jnp.where(listed, base + turn, NEG)
        s_zero = jnp.where(first, last - quad, NEG)
        peak = jnp.max(jnp.maximum(jnp.maximum(s_plus, s_minus), s_zero), axis=0, keepdims=True)
        peak = jnp.maximum(peak, pltpu.roll(peak, 32, 1))
        peak = jnp.maximum(peak, pltpu.roll(peak, 64, 1))
        e_plus = jnp.where(listed, jnp.exp(s_plus - peak), 0.0)
        e_minus = jnp.where(listed, jnp.exp(s_minus - peak), 0.0)
        e_zero = jnp.where(first, jnp.exp(s_zero - peak), 0.0)
        total = jnp.sum(e_plus + e_minus + e_zero, axis=0, keepdims=True)
        total = total + pltpu.roll(total, 32, 1)
        total = total + pltpu.roll(total, 64, 1)
        inv = 1.0 / total
        both = (e_plus + e_minus) * inv
        gap = (e_plus - e_minus) * inv
        zero = e_zero * inv
        blank = jnp.zeros((64, 128), F32)
        for k, (a, b) in enumerate(
            ((both, blank), (blank, -gap), (blank, both), (gap, blank), (zero, pltpu.roll(zero, 32, 1)))
        ):
            cscr[k, even, :] = a
            cscr[k, odd, :] = b
        share = dot(both + zero, ohb, NT, HIGH)
        bsscr[even, :] = share
        bsscr[odd, :] = blank
        coef = jnp.concatenate([cscr[k] for k in range(5)], axis=1)[:, 0:576].astype(BF16)
        dbuf[:, :, half : half + 128] = bsscr[...].reshape(NODES, ROWS, 128).astype(BF16)

        def rspan(q):
            return slice(q * width, (q + 1) * width + (128 if q == COLOURS - 1 else 0))

        def rs(q, k, t):
            return pltpu.make_async_remote_copy(
                src_ref=dbuf.at[k, :, rspan(q)], dst_ref=rsb.at[k, :, rspan(q)],
                send_sem=rs_s.at[0],
                recv_sem=rs_b.at[q] if k == t else rs_a.at[q, STAGES[q][0].index(k ^ t)],
                device_id=dev(t, core), device_id_type=MESH,
            )

        def collect(q, k, froms):
            acc = dbuf[k, :, rspan(q)].astype(F32)
            arrival = rs_a.at[q, STAGES[q][0].index(k)] if k else rs_b.at[q]
            settle(rsb.at[1 : 1 + len(froms), :, rspan(q)], rs_s.at[0], arrival).wait_recv()
            for child in froms:
                acc = acc + rsb[child, :, rspan(q)].astype(F32)
            return acc

        for q in range(COLOURS):
            out = dot(coef, rbuf[:, span(q)])
            dbuf[:, :, span(q)] = out.reshape(NODES, ROWS, width).astype(BF16)
            for k in STAGES[q][0] + (0,):
                for t in STAGES[q][1][::-1]:
                    rs(q, k ^ t, t).start()

        lid = lax.broadcasted_iota(jnp.int32, (groups, lines), 0)
        tri = (
            lax.broadcasted_iota(jnp.int32, (lines, lines), 0)
            < lax.broadcasted_iota(jnp.int32, (lines, lines), 1)
        ).astype(F32)
        wide = (
            lax.broadcasted_iota(jnp.int32, (lines, lines * ROWS), 1) // ROWS
            == lax.broadcasted_iota(jnp.int32, (lines, lines * ROWS), 0)
        ).astype(F32)
        wide16 = (
            lax.broadcasted_iota(jnp.int32, (lines, lines * BINS), 1) // BINS
            == lax.broadcasted_iota(jnp.int32, (lines, lines * BINS), 0)
        ).astype(F32)
        keys = []
        for j in range(2):
            row = slabv[j : j + 1, :]
            own = jnp.zeros((1, lines), jnp.int32)
            for s in range(groups):
                own = own + jnp.where(row == s, owners[0, s], 0)
            hit = (lid == own).astype(F32)
            rank = jnp.sum(hit * dot(hit, tri), axis=0, keepdims=True)
            keys.append((own * 8).astype(F32) + rank)
        key8 = [dot(k, wide) for k in keys]
        col = lax.broadcasted_iota(jnp.int32, (1, lines * ROWS), 1) % ROWS
        pick = jnp.where(col % 4 >= 2, key8[1], key8[0]).astype(jnp.int32) * 8 + col
        rid = lax.broadcasted_iota(jnp.int32, (groups * slots, lines * ROWS), 0)
        inner = rid % slots
        r4 = (
            (inner >= CAP).astype(jnp.int32)
            + (inner >= 2 * CAP).astype(jnp.int32)
            + (inner >= 3 * CAP).astype(jnp.int32)
            + (inner >= 4 * CAP).astype(jnp.int32)
        )
        want = ((rid // slots) * 8 + (inner - CAP * r4)) * 8 + 4 * core + r4
        sel[...] = (want == pick).astype(F32).astype(BF16)
        for j in range(2):
            wkey[8 * j : 8 * j + 8, :] = jnp.broadcast_to(dot(keys[j], wide16), (8, lines * BINS))

        for i in range(3):
            for q in range(COLOURS):
                k = STAGES[q][0][i]
                acc = collect(q, k, [k ^ t for t in STAGES[q][1]])
                dbuf[k, :, rspan(q)] = acc.astype(BF16)
                rs(q, k, k).start()

        def squares(i, carry):
            v = tabf[:, pl.ds(pl.multiple_of(i * LINE, LINE), LINE)].astype(F32)
            w3[pl.ds(pl.multiple_of(i * BINS, BINS), BINS), :] = v * v
            return carry

        lax.fori_loop(0, lines, squares, 0)
        spread_word(2)
        extra = None
        for q in range(COLOURS):
            acc = collect(q, 0, STAGES[q][1] + STAGES[q][0])
            zb[core, :, span(q)] = acc[:, :width].astype(BF16)
            if q == COLOURS - 1:
                extra = acc[:, width:]
        zx = pltpu.make_async_remote_copy(
            src_ref=zb.at[core], dst_ref=zb.at[core], send_sem=zx_sem.at[0], recv_sem=zx_sem.at[1],
            device_id=mate, device_id_type=MESH,
        )
        push(zx)

        rows8 = lax.broadcasted_iota(jnp.int32, (8, 128), 0)
        for j in range(2):
            wzs[j : j + 1, :] = jnp.sum(
                jnp.where(rows8 == 4 * core + 2 * j, extra, 0.0), axis=0, keepdims=True
            )
        order = sorted(range(1, groups), key=lambda k: -min(k, groups - k))

        def wmsg(k):
            return pltpu.make_async_remote_copy(
                src_ref=wzs, dst_ref=wzr.at[k], send_sem=w_sem.at[0], recv_sem=w_sem.at[1],
                device_id=((z + k) % groups, d), device_id_type=MESH,
            )

        def zmsg(k):
            return pltpu.make_async_remote_copy(
                src_ref=zsend.at[(z + k) % groups, 0 : 4 * CAP], dst_ref=zrecv.at[k, 0 : 4 * CAP],
                send_sem=z_sem.at[0], recv_sem=z_sem.at[1],
                device_id=((z + k) % groups, d), device_id_type=MESH,
            )

        for k in order:
            wmsg(k).start()
        zx.wait_recv()
        stack = jnp.concatenate(
            [
                zb[h, :, LINE * i : LINE * i + LINE].astype(F32)
                for h in range(2)
                for i in range(hl)
            ],
            axis=0,
        ).astype(BF16)
        packed = dot(sel[...], stack)
        zsend[...] = packed.astype(BF16).reshape(groups, slots, LINE)
        for k in order:
            zmsg(k).start()
        acc_w = wzs[...]
        settle(wzr.at[1:groups], w_sem.at[0], w_sem.at[1]).wait_recv()
        for k in range(1, groups):
            acc_w = acc_w + wzr[k]
        spread = (
            lax.broadcasted_iota(jnp.int32, (128, lines * BINS), 1) % BINS
            == lax.broadcasted_iota(jnp.int32, (128, lines * BINS), 0)
        ).astype(F32)
        scale = 64.0 / (16 * groups * NODES * 2)
        tall = jnp.concatenate(
            [jnp.broadcast_to(acc_w[j : j + 1, :] * scale, (8, 128)) for j in range(2)], axis=0
        )
        coefw = dot(tall, spread, NN, HIGH)
        slot = lax.broadcasted_iota(jnp.int32, (16, lines * BINS), 0) % 8
        ok = wkey[...].astype(jnp.int32) == z * 8 + slot
        weights = dot(jnp.where(ok, coefw, 0.0), w3[...], NN, HIGH)
        for j in range(2):
            for c in range(CAP):
                o_weight[c, j : j + 1, :] = weights[8 * j + c : 8 * j + c + 1, :]
        acc = zsend[z, 0 : 4 * CAP].astype(F32)
        settle(zrecv.at[1:groups, 0 : 4 * CAP], z_sem.at[0], z_sem.at[1]).wait_recv()
        for k in range(1, groups):
            acc = acc + zrecv[k, 0 : 4 * CAP].astype(F32)
        for r in range(4):
            for c in range(CAP):
                o_data[r // 2, c, r % 2 : r % 2 + 1, :] = acc[CAP * r + c : CAP * r + c + 1, :]

        for c in sent:
            c.wait_send()
        settle(pbuf.at[1:NODES], ag_s.at[0], ag_l.at[0]).wait_send()
        settle(dbuf.at[1:NODES], rs_s.at[0], rs_b.at[0]).wait_send()
        settle(wzr.at[1:groups], w_sem.at[0], w_sem.at[1]).wait_send()
        settle(zrecv.at[1:groups, 0 : 4 * CAP], z_sem.at[0], z_sem.at[1]).wait_send()

    return kernel


def body(particles, defocus_bin, candidates, projections, ctf_table, inv_noise, line_slab, slab_owner):
    groups = lax.axis_size("grp")
    pixels = particles.shape[2]
    lines = pixels // LINE
    half = pixels // 2
    trig = jnp.asarray(phase_rows(lines))
    hbm = pl.BlockSpec(memory_space=pltpu.HBM)
    vmem = pl.BlockSpec(memory_space=pltpu.VMEM)
    dma = pltpu.SemaphoreType.DMA
    data, weight = pl.pallas_call(
        make_kernel(lines, groups),
        name="estep",
        out_shape=(
            jax.ShapeDtypeStruct((2, CAP, 2, LINE), F32),
            jax.ShapeDtypeStruct((CAP, 2, LINE), F32),
        ),
        in_specs=[hbm] * 9,
        out_specs=(vmem, vmem),
        scratch_shapes=[
            pltpu.VMEM((2, 16, 2, half), BF16),
            pltpu.VMEM((half // CHUNKS // LINE, 32, LINE), F32),
            pltpu.VMEM((16, half), F32),
            pltpu.VMEM((2, 8, 16), jnp.int32),
            pltpu.VMEM((2, 1, 16), jnp.int32),
            pltpu.VMEM((2, lines), jnp.int32),
            pltpu.SMEM((1, groups), jnp.int32),
            pltpu.VMEM((8, half), F32),
            pltpu.VMEM((BINS, half), BF16),
            pltpu.VMEM((BINS, pixels), BF16),
            pltpu.VMEM((1, half), F32),
            pltpu.VMEM((2 * BINS, half), BF16),
            pltpu.VMEM((NODES, 2, 2, 2, half), BF16),
            pltpu.VMEM((128, half // COLOURS), F32),
            pltpu.VMEM((576, half), BF16),
            pltpu.VMEM((5, 128, 128), F32),
            pltpu.VMEM((128, 128), F32),
            pltpu.VMEM((2, 3, 64, 128), F32),
            pltpu.VMEM((5, 128, 128), F32),
            pltpu.VMEM((128, 128), F32),
            pltpu.VMEM((NODES, ROWS, half + 128), BF16),
            pltpu.VMEM((NODES, ROWS, half + 128), BF16),
            pltpu.VMEM((2, ROWS, half), BF16),
            pltpu.VMEM((groups * 32, lines * ROWS), BF16),
            pltpu.VMEM((16, lines * BINS), F32),
            pltpu.VMEM((lines * BINS, LINE), F32),
            pltpu.VMEM((groups, 32, LINE), BF16),
            pltpu.VMEM((groups, 32, LINE), BF16),
            pltpu.VMEM((2, 128), F32),
            pltpu.VMEM((groups, 2, 128), F32),
            dma((10,)), dma((4,)), dma((4,)),
            dma((1,)), dma((COLOURS, 3)), dma((COLOURS,)), dma((COLOURS,)),
            dma((1,)), dma((COLOURS, 3)), dma((COLOURS,)),
            dma((2,)), dma((2,)), dma((2,)), dma((2,)),
            pltpu.SemaphoreType.REGULAR((3,)),
        ],
        compiler_params=pltpu.CompilerParams(
            collective_id=0, has_side_effects=True, vmem_limit_bytes=67043328
        ),
    )(
        particles,
        projections,
        ctf_table,
        inv_noise.reshape(1, pixels),
        trig,
        candidates.T,
        defocus_bin.reshape(1, 16),
        line_slab,
        slab_owner.reshape(1, groups),
    )
    return (jnp.transpose(data, (0, 2, 1, 3))[None], jnp.transpose(weight, (1, 0, 2))[None])


def solution(mesh):
    return jax.shard_map(
        body,
        mesh=mesh,
        in_specs=(
            P(("grp", "dev"), None, None),
            P(("grp", "dev")),
            P(("grp", "dev"), None),
            P("dev", None, None),
            P(),
            P(),
            P("dev", None),
            P(),
        ),
        out_specs=(P("grp", "dev", None, None, None), P("grp", "dev", None, None)),
        check_vma=False,
    )
```

```python
import math

import jax
import jax.numpy as jnp
import numpy as np
from jax import lax
from jax.experimental import pallas as pl
from jax.experimental.pallas import tpu as pltpu
from jax.sharding import PartitionSpec as P

LINE = 128
CAP = 6
BINS = 16
NODES = 16
COLOURS = 2
CHUNKS = 4
ROWS = 8
NEG = -3.0e38
MESH = pl.DeviceIdType.MESH
F32 = jnp.float32
BF16 = jnp.bfloat16
HIGH = lax.Precision.HIGHEST
NN = (((1,), (0,)), ((), ()))
NT = (((1,), (1,)), ((), ()))
TN = (((0,), (0,)), ((), ()))
STAGES = (
    ((1, 4, 5), (3, 12, 15)),
    ((3, 12, 15), (1, 4, 5)),
)
NEAR = (1, 3, 4, 12, 5, 15)


def dot(a, b, dims=NN, precision=None):
    return lax.dot_general(a, b, dims, preferred_element_type=F32, precision=precision)


def phase_rows(lines):
    line = np.repeat(np.arange(lines), LINE).astype(np.float64)
    column = np.tile(np.arange(LINE), lines)
    freq = np.where(column < LINE // 2, column, column - LINE).astype(np.float64)
    moves = ((0, 1), (1, -1), (1, 0), (1, 1))
    angle = np.stack([dx * line + dy * freq for dx, dy in moves]) * (2.0 * math.pi / LINE)
    return np.concatenate([np.cos(angle), np.sin(angle)]).astype(np.float32)


def flip(v, k):
    if k == 0:
        return v
    if k == 1:
        return v + 1 - 2 * (v % 2)
    if k == 2:
        return (v + 2) % 4
    return 3 - v


def make_kernel(lines, groups):
    half = lines * LINE // 2
    width = half // COLOURS
    hl = lines // 2
    piece = half // CHUNKS
    slots = 32

    def kernel(parts, proj, table, noise, trig, cand, bins, slab, owner,
               o_data, o_weight,
               xin, xs, ctfv, candb, binb, slabv, owners, trigv, tabh, tabf, noisev, nsv, pbuf, ps, rbuf,
               gscr, bpscr, sx, cscr, bsscr, dbuf, rsb, zb, sel, wkey, w3, zsend, zrecv, wzs, wzr,
               loc, ex_s, ex_r, ag_s, ag_a, ag_b, ag_l, rs_s, rs_a, rs_b, sx_sem, zx_s, zx_r, z_sem, w_sem, ring):
        z = lax.axis_index("grp")
        d = lax.axis_index("dev")
        core = d % 2
        node = d // 2
        nx, ny = node % 4, node // 4
        other = 1 - core

        def dev(k, c):
            return (z, (flip(ny, k // 4) * 4 + flip(nx, k % 4)) * 2 + c)

        def along(k):
            return ((z + k + groups) % groups, d)

        mate = (z, node * 2 + other)

        def greet(sem, to):
            pl.semaphore_signal(sem, inc=1, device_id=to, device_id_type=MESH)

        barrier = pltpu.get_barrier_semaphore()
        greet(barrier, mate)
        for k in NEAR:
            greet(barrier, dev(k, core))
            greet(barrier, dev(k, other))
        greet(barrier, along(1))
        greet(barrier, along(-1))

        mine = pl.multiple_of(core * half, LINE)
        theirs = pl.multiple_of(other * half, LINE)
        loads = [
            pltpu.make_async_copy(bins, binb.at[core], loc.at[0]),
            pltpu.make_async_copy(table.at[:, pl.ds(mine, half)], tabh, loc.at[1]),
            pltpu.make_async_copy(parts.at[:, :, pl.ds(mine, half)], xin.at[core], loc.at[2]),
            pltpu.make_async_copy(trig.at[:, pl.ds(mine, half)], trigv, loc.at[3]),
            pltpu.make_async_copy(proj.at[:, :, pl.ds(mine, half)], pbuf.at[0, core], loc.at[4]),
            pltpu.make_async_copy(noise.at[:, pl.ds(mine, half)], noisev, loc.at[5]),
            pltpu.make_async_copy(cand, candb.at[core], loc.at[6]),
            pltpu.make_async_copy(slab, slabv, loc.at[7]),
            pltpu.make_async_copy(table, tabf, loc.at[8]),
            pltpu.make_async_copy(owner, owners, loc.at[9]),
        ]
        for c in loads:
            c.start()

        pl.semaphore_wait(barrier, 3 + 2 * len(NEAR))

        def span(q):
            return slice(q * width, (q + 1) * width)

        def cast(q, t, c):
            side = pl.multiple_of((mine if c is core else theirs) + q * width, LINE)
            return pltpu.make_async_remote_copy(
                src_ref=proj.at[:, :, pl.ds(side, width)],
                dst_ref=pbuf.at[t, core, :, :, span(q)],
                send_sem=ag_s.at[0],
                recv_sem=ag_a.at[q, STAGES[q][0].index(t)] if t in STAGES[q][0] else ag_b.at[q],
                device_id=dev(t, c), device_id_type=MESH,
            )

        def relay(q, k, s, t):
            return pltpu.make_async_remote_copy(
                src_ref=pbuf.at[k, s, :, :, span(q)], dst_ref=pbuf.at[k ^ t, s, :, :, span(q)],
                send_sem=ag_s.at[0], recv_sem=ag_l.at[q],
                device_id=dev(t, core), device_id_type=MESH,
            )

        def settle(ref, send, recv):
            return pltpu.make_async_remote_copy(
                src_ref=ref, dst_ref=ref, send_sem=send, recv_sem=recv, device_id=mate, device_id_type=MESH,
            )

        sent = []

        def push(c):
            c.start()
            sent.append(c)

        for stage in range(2):
            for i in (2, 0, 1):
                for q in range(COLOURS):
                    cast(q, STAGES[q][stage][i], core).start()
                    cast(q, STAGES[q][stage][i], other).start()
        swaps = [
            pltpu.make_async_remote_copy(
                src_ref=src, dst_ref=dst, send_sem=ex_s.at[i], recv_sem=ex_r.at[i],
                device_id=mate, device_id_type=MESH,
            )
            for i, (src, dst) in enumerate(
                (
                    (proj.at[:, :, pl.ds(theirs, half)], pbuf.at[0, core]),
                    (bins, binb.at[core]),
                    (cand, candb.at[core]),
                    (parts.at[:, :, pl.ds(theirs, half)], xin.at[core]),
                )
            )
        ]
        for c in swaps:
            push(c)
        reach = 1
        rounds = []
        while 2 * reach <= groups // 2:
            rounds.append(reach)
            reach *= 2
        if rounds:
            greet(ring.at[0], along(1))
            greet(ring.at[0], along(-1))

        def spread_word(i):
            if i < len(rounds):
                pl.semaphore_wait(ring.at[i], 2)
                if i + 1 < len(rounds):
                    greet(ring.at[i + 1], along(rounds[i + 1]))
                    greet(ring.at[i + 1], along(-rounds[i + 1]))

        even2, odd2 = pl.ds(0, 16, stride=2), pl.ds(1, 16, stride=2)
        bid = lax.broadcasted_iota(jnp.int32, (BINS, 16), 0)

        def rotate(s):
            hot = (bid == binb[s]).astype(F32).astype(BF16)
            ctfv[...] = dot(hot, tabh[...], TN)

            def chunk(i, carry):
                for t in range(piece // LINE):
                    at_ = pl.ds(pl.multiple_of(i * piece + t * LINE, LINE), LINE)
                    for p in range(16):
                        xs[t, 2 * p : 2 * p + 2, :] = xin[s, p, :, at_].astype(F32)
                    for part in range(2):
                        x = ctfv[:, at_] * xs[t, even2 if part == 0 else odd2, :]
                        r0 = pl.multiple_of(512 + part * 32 + s * 16, 16)
                        rbuf[pl.ds(r0, 16), at_] = x.astype(BF16)
                        for u in range(8):
                            r0 = pl.multiple_of(part * 256 + u * 32 + s * 16, 16)
                            rbuf[pl.ds(r0, 16), at_] = (x * trigv[u : u + 1, at_]).astype(BF16)
                return carry

            lax.fori_loop(0, CHUNKS, chunk, 0)

        for i in range(4):
            loads[i].wait()
        rotate(core)
        for i in range(3):
            for q in range(COLOURS):
                k = STAGES[q][0][i]
                settle(pbuf.at[k, :, :, :, span(q)], ag_s.at[0], ag_a.at[q, i]).wait_recv()
                for t in STAGES[q][1][::-1]:
                    for s in range(2):
                        relay(q, k, s, t).start()
        swaps[1].wait_recv()
        swaps[3].wait_recv()
        rotate(other)

        for i in range(4, 10):
            loads[i].wait()
        swaps[2].wait_recv()
        lanes = lax.broadcasted_iota(jnp.int32, (1, 128), 1)
        cid = lax.broadcasted_iota(jnp.int32, (128, 128), 0)
        lane_core = (lanes % 32) // 16
        til = (
            lax.broadcasted_iota(jnp.int32, (16, 128), 1) % 16
            == lax.broadcasted_iota(jnp.int32, (16, 128), 0)
        ).astype(F32)
        bl = [dot(binb[s].astype(F32), til) for s in range(2)]
        blane = jnp.where(lane_core == 1, bl[1], bl[0]).astype(jnp.int32)
        ohb = (cid == blane).astype(F32)
        cl = [dot(candb[s].astype(F32), til) for s in range(2)]
        clane = jnp.where(lane_core == 1, cl[1], cl[0]).astype(jnp.int32)
        rid = lax.broadcasted_iota(jnp.int32, (64, 128), 0)
        jid = ((rid // 4) ^ node) * 4 + rid % 4
        listed = jid == clane[0:1, :]
        for k in range(1, 8):
            listed = jnp.logical_or(listed, jid == clane[k : k + 1, :])
        t32 = tabh[...].astype(F32)
        ns32 = t32 * t32 * noisev[...]
        ns_hi = ns32.astype(BF16)
        nsv[0:BINS, :] = ns_hi
        nsv[BINS : 2 * BINS, :] = (ns32 - ns_hi.astype(F32)).astype(BF16)
        bpscr[...] = jnp.zeros(bpscr.shape, F32)
        gscr[...] = jnp.zeros(gscr.shape, F32)

        def score(q, ks):
            for i, k in enumerate(ks):
                for s in range(2):
                    for j in range(2):
                        r = 8 * i + 4 * s + 2 * j
                        ps[r : r + 2, :] = pbuf[k, s, j, :, span(q)].astype(F32)
            p32 = ps[0 : 8 * len(ks), :]
            nz = noisev[:, span(q)]
            got = dot((p32 * nz).astype(BF16), rbuf[:, span(q)], NT)
            pp = p32 * p32
            pp_hi = pp.astype(BF16)
            pp_lo = (pp - pp_hi.astype(F32)).astype(BF16)
            ns = nsv[:, span(q)]
            power = dot(pp_hi, ns, NT)
            power = power[:, 0:BINS] + power[:, BINS : 2 * BINS] + dot(pp_lo, ns[0:BINS], NT)
            for i, k in enumerate(ks):
                here, there = slice(8 * i, 8 * i + 8), slice(8 * k, 8 * k + 8)
                bpscr[there, 0:BINS] += power[here, :]
                for b in range(5):
                    w = min(128, 576 - 128 * b)
                    gscr[b, there, 0:w] += got[here, 128 * b : 128 * b + w]

        swaps[0].wait_recv()
        for q in range(COLOURS):
            settle(pbuf.at[1:4, :, :, :, span(q)], ag_s.at[0], ag_b.at[q]).wait_recv()
            score(q, (0,) + STAGES[q][0] + STAGES[q][1])
        spread_word(0)
        for q in range(COLOURS):
            late = tuple(a ^ b for a in STAGES[q][0] for b in STAGES[q][1])
            settle(pbuf.at[1:10, :, :, :, span(q)], ag_s.at[0], ag_l.at[q]).wait_recv()
            score(q, late)
        even, odd = pl.ds(0, 64, stride=2), pl.ds(1, 64, stride=2)
        ge = [gscr[k, even, :] for k in range(5)]
        go = [gscr[k, odd, :] for k in range(5)]
        sx[core, 0] = ge[0] + go[2]
        sx[core, 1] = go[1] - ge[3]
        sx[core, 2] = jnp.where(
            lanes < 32, ge[4] + pltpu.roll(go[4], 96, 1), pltpu.roll(bpscr[even, :] + bpscr[odd, :], 64, 1)
        )
        trade = pltpu.make_async_remote_copy(
            src_ref=sx.at[core], dst_ref=sx.at[core], send_sem=sx_sem.at[0], recv_sem=sx_sem.at[1],
            device_id=mate, device_id_type=MESH,
        )
        push(trade)
        spread_word(1)
        trade.wait_recv()

        last = sx[0, 2] + sx[1, 2]
        power = jnp.where(lanes < BINS, pltpu.roll(last, 64, 1), 0.0)
        quad = 0.5 * dot(power, ohb, NN, HIGH)
        base = sx[0, 0] + sx[1, 0] - quad
        turn = sx[0, 1] + sx[1, 1]
        first = jnp.logical_and(listed, lanes < 32)
        s_plus = jnp.where(listed, base - turn, NEG)
        s_minus = jnp.where(listed, base + turn, NEG)
        s_zero = jnp.where(first, last - quad, NEG)
        peak = jnp.max(jnp.maximum(jnp.maximum(s_plus, s_minus), s_zero), axis=0, keepdims=True)
        peak = jnp.maximum(peak, pltpu.roll(peak, 32, 1))
        peak = jnp.maximum(peak, pltpu.roll(peak, 64, 1))
        e_plus = jnp.where(listed, jnp.exp(s_plus - peak), 0.0)
        e_minus = jnp.where(listed, jnp.exp(s_minus - peak), 0.0)
        e_zero = jnp.where(first, jnp.exp(s_zero - peak), 0.0)
        total = jnp.sum(e_plus + e_minus + e_zero, axis=0, keepdims=True)
        total = total + pltpu.roll(total, 32, 1)
        total = total + pltpu.roll(total, 64, 1)
        inv = 1.0 / total
        both = (e_plus + e_minus) * inv
        gap = (e_plus - e_minus) * inv
        zero = e_zero * inv
        blank = jnp.zeros((64, 128), F32)
        for k, (a, b) in enumerate(
            ((both, blank), (blank, -gap), (blank, both), (gap, blank), (zero, pltpu.roll(zero, 32, 1)))
        ):
            cscr[k, even, :] = a
            cscr[k, odd, :] = b
        coef = jnp.concatenate([cscr[k] for k in range(5)], axis=1)[:, 0:576].astype(BF16)

        def rspan(q):
            return slice(q * width, (q + 1) * width + (128 if q == COLOURS - 1 else 0))

        def rs(q, k, t):
            return pltpu.make_async_remote_copy(
                src_ref=dbuf.at[k, :, rspan(q)], dst_ref=rsb.at[k, :, rspan(q)],
                send_sem=rs_s.at[0],
                recv_sem=rs_b.at[q] if k == t else rs_a.at[q, STAGES[q][0].index(k ^ t)],
                device_id=dev(t, core), device_id_type=MESH,
            )

        def collect(q, k, froms):
            acc = dbuf[k, :, rspan(q)].astype(F32)
            arrival = rs_a.at[q, STAGES[q][0].index(k)] if k else rs_b.at[q]
            settle(rsb.at[1 : 1 + len(froms), :, rspan(q)], rs_s.at[0], arrival).wait_recv()
            for child in froms:
                acc = acc + rsb[child, :, rspan(q)].astype(F32)
            return acc

        for q in range(COLOURS):
            if q == COLOURS - 1:
                share = dot(both + zero, ohb, NT, HIGH)
                bsscr[even, :] = share
                bsscr[odd, :] = blank
                dbuf[:, :, half : half + 128] = bsscr[...].reshape(NODES, ROWS, 128).astype(BF16)
            out = dot(coef, rbuf[:, span(q)])
            dbuf[:, :, span(q)] = out.reshape(NODES, ROWS, width).astype(BF16)
            for k in STAGES[q][0][::-1] + (0,):
                for t in STAGES[q][1][::-1]:
                    rs(q, k ^ t, t).start()

        lid = lax.broadcasted_iota(jnp.int32, (groups, lines), 0)
        tri = (
            lax.broadcasted_iota(jnp.int32, (lines, lines), 0)
            < lax.broadcasted_iota(jnp.int32, (lines, lines), 1)
        ).astype(F32)
        place = lax.broadcasted_iota(jnp.int32, (lines, lines * ROWS), 1) // ROWS
        place = jnp.where(place < hl, place + core * hl, place - core * hl)
        wide = (place == lax.broadcasted_iota(jnp.int32, (lines, lines * ROWS), 0)).astype(F32)
        wide16 = (
            lax.broadcasted_iota(jnp.int32, (lines, lines * BINS), 1) // BINS
            == lax.broadcasted_iota(jnp.int32, (lines, lines * BINS), 0)
        ).astype(F32)
        keys = []
        for j in range(2):
            row = slabv[j : j + 1, :]
            own = jnp.zeros((1, lines), jnp.int32)
            for s in range(groups):
                own = own + jnp.where(row == s, owners[0, s], 0)
            hit = (lid == own).astype(F32)
            rank = jnp.sum(hit * dot(hit, tri), axis=0, keepdims=True)
            keys.append((own * 8).astype(F32) + rank)
        key8 = [dot(k, wide) for k in keys]
        col = lax.broadcasted_iota(jnp.int32, (1, lines * ROWS), 1) % ROWS
        pick = jnp.where(col % 4 >= 2, key8[1], key8[0]).astype(jnp.int32) * 8 + col
        rid = lax.broadcasted_iota(jnp.int32, (groups * slots, lines * ROWS), 0)
        inner = rid % slots
        r4 = (
            (inner >= CAP).astype(jnp.int32)
            + (inner >= 2 * CAP).astype(jnp.int32)
            + (inner >= 3 * CAP).astype(jnp.int32)
            + (inner >= 4 * CAP).astype(jnp.int32)
        )
        want = ((rid // slots) * 8 + (inner - CAP * r4)) * 8 + 4 * core + r4
        sel[...] = (want == pick).astype(F32).astype(BF16)
        for j in range(2):
            wkey[8 * j : 8 * j + 8, :] = jnp.broadcast_to(dot(keys[j], wide16), (8, lines * BINS))

        for i in (2, 1, 0):
            for q in range(COLOURS):
                k = STAGES[q][0][i]
                acc = collect(q, k, [k ^ t for t in STAGES[q][1]])
                dbuf[k, :, rspan(q)] = acc.astype(BF16)
                rs(q, k, k).start()

        def squares(i, carry):
            v = tabf[:, pl.ds(pl.multiple_of(i * LINE, LINE), LINE)].astype(F32)
            w3[pl.ds(pl.multiple_of(i * BINS, BINS), BINS), :] = v * v
            return carry

        lax.fori_loop(0, lines, squares, 0)
        spread_word(2)
        def zx(q):
            return pltpu.make_async_remote_copy(
                src_ref=zb.at[core, :, span(q)], dst_ref=zb.at[core, :, span(q)],
                send_sem=zx_s.at[q], recv_sem=zx_r.at[q], device_id=mate, device_id_type=MESH,
            )

        extra = None
        for q in range(COLOURS):
            acc = collect(q, 0, STAGES[q][1] + STAGES[q][0])
            zb[core, :, span(q)] = acc[:, :width].astype(BF16)
            push(zx(q))
            if q == COLOURS - 1:
                extra = acc[:, width:]

        rows8 = lax.broadcasted_iota(jnp.int32, (8, 128), 0)
        for j in range(2):
            wzs[j : j + 1, :] = jnp.sum(
                jnp.where(rows8 == 4 * core + 2 * j, extra, 0.0), axis=0, keepdims=True
            )
        order = sorted(range(1, groups), key=lambda k: -min(k, groups - k))

        def wmsg(k):
            return pltpu.make_async_remote_copy(
                src_ref=wzs, dst_ref=wzr.at[k], send_sem=w_sem.at[0], recv_sem=w_sem.at[1],
                device_id=((z + k) % groups, d), device_id_type=MESH,
            )

        def zmsg(k):
            return pltpu.make_async_remote_copy(
                src_ref=zsend.at[(z + k) % groups, 0 : 4 * CAP], dst_ref=zrecv.at[k, 0 : 4 * CAP],
                send_sem=z_sem.at[0], recv_sem=z_sem.at[1],
                device_id=((z + k) % groups, d), device_id_type=MESH,
            )

        for k in order:
            wmsg(k).start()
        def stack(h):
            return jnp.concatenate(
                [zb[h, :, LINE * i : LINE * i + LINE].astype(F32) for i in range(hl)], axis=0
            ).astype(BF16)

        packed = dot(sel[:, 0 : hl * ROWS], stack(core))
        for q in range(COLOURS):
            zx(q).wait_recv()
        packed = packed + dot(sel[:, hl * ROWS :], stack(other))
        zsend[...] = packed.astype(BF16).reshape(groups, slots, LINE)
        for k in order:
            zmsg(k).start()
        acc_w = wzs[...]
        settle(wzr.at[1:groups], w_sem.at[0], w_sem.at[1]).wait_recv()
        for k in range(1, groups):
            acc_w = acc_w + wzr[k]
        spread = (
            lax.broadcasted_iota(jnp.int32, (128, lines * BINS), 1) % BINS
            == lax.broadcasted_iota(jnp.int32, (128, lines * BINS), 0)
        ).astype(F32)
        scale = 64.0 / (16 * groups * NODES * 2)
        tall = jnp.concatenate(
            [jnp.broadcast_to(acc_w[j : j + 1, :] * scale, (8, 128)) for j in range(2)], axis=0
        )
        coefw = dot(tall, spread, NN, HIGH)
        slot = lax.broadcasted_iota(jnp.int32, (16, lines * BINS), 0) % 8
        ok = wkey[...].astype(jnp.int32) == z * 8 + slot
        weights = dot(jnp.where(ok, coefw, 0.0), w3[...], NN, HIGH)
        for j in range(2):
            for c in range(CAP):
                o_weight[c, j : j + 1, :] = weights[8 * j + c : 8 * j + c + 1, :]
        acc = zsend[z, 0 : 4 * CAP].astype(F32)
        settle(zrecv.at[1:groups, 0 : 4 * CAP], z_sem.at[0], z_sem.at[1]).wait_recv()
        for k in range(1, groups):
            acc = acc + zrecv[k, 0 : 4 * CAP].astype(F32)
        for r in range(4):
            for c in range(CAP):
                o_data[r // 2, c, r % 2 : r % 2 + 1, :] = acc[CAP * r + c : CAP * r + c + 1, :]

        for c in sent:
            c.wait_send()
        settle(pbuf.at[1:NODES], ag_s.at[0], ag_l.at[0]).wait_send()
        settle(dbuf.at[1:NODES], rs_s.at[0], rs_b.at[0]).wait_send()
        settle(wzr.at[1:groups], w_sem.at[0], w_sem.at[1]).wait_send()
        settle(zrecv.at[1:groups, 0 : 4 * CAP], z_sem.at[0], z_sem.at[1]).wait_send()

    return kernel


def body(particles, defocus_bin, candidates, projections, ctf_table, inv_noise, line_slab, slab_owner):
    groups = lax.axis_size("grp")
    pixels = particles.shape[2]
    lines = pixels // LINE
    half = pixels // 2
    trig = jnp.asarray(phase_rows(lines))
    hbm = pl.BlockSpec(memory_space=pltpu.HBM)
    vmem = pl.BlockSpec(memory_space=pltpu.VMEM)
    dma = pltpu.SemaphoreType.DMA
    data, weight = pl.pallas_call(
        make_kernel(lines, groups),
        name="estep",
        out_shape=(
            jax.ShapeDtypeStruct((2, CAP, 2, LINE), F32),
            jax.ShapeDtypeStruct((CAP, 2, LINE), F32),
        ),
        in_specs=[hbm] * 9,
        out_specs=(vmem, vmem),
        scratch_shapes=[
            pltpu.VMEM((2, 16, 2, half), BF16),
            pltpu.VMEM((half // CHUNKS // LINE, 32, LINE), F32),
            pltpu.VMEM((16, half), F32),
            pltpu.VMEM((2, 8, 16), jnp.int32),
            pltpu.VMEM((2, 1, 16), jnp.int32),
            pltpu.VMEM((2, lines), jnp.int32),
            pltpu.SMEM((1, groups), jnp.int32),
            pltpu.VMEM((8, half), F32),
            pltpu.VMEM((BINS, half), BF16),
            pltpu.VMEM((BINS, pixels), BF16),
            pltpu.VMEM((1, half), F32),
            pltpu.VMEM((2 * BINS, half), BF16),
            pltpu.VMEM((NODES, 2, 2, 2, half), BF16),
            pltpu.VMEM((128, half // COLOURS), F32),
            pltpu.VMEM((576, half), BF16),
            pltpu.VMEM((5, 128, 128), F32),
            pltpu.VMEM((128, 128), F32),
            pltpu.VMEM((2, 3, 64, 128), F32),
            pltpu.VMEM((5, 128, 128), F32),
            pltpu.VMEM((128, 128), F32),
            pltpu.VMEM((NODES, ROWS, half + 128), BF16),
            pltpu.VMEM((NODES, ROWS, half + 128), BF16),
            pltpu.VMEM((2, ROWS, half), BF16),
            pltpu.VMEM((groups * 32, lines * ROWS), BF16),
            pltpu.VMEM((16, lines * BINS), F32),
            pltpu.VMEM((lines * BINS, LINE), F32),
            pltpu.VMEM((groups, 32, LINE), BF16),
            pltpu.VMEM((groups, 32, LINE), BF16),
            pltpu.VMEM((2, 128), F32),
            pltpu.VMEM((groups, 2, 128), F32),
            dma((10,)), dma((4,)), dma((4,)),
            dma((1,)), dma((COLOURS, 3)), dma((COLOURS,)), dma((COLOURS,)),
            dma((1,)), dma((COLOURS, 3)), dma((COLOURS,)),
            dma((2,)), dma((COLOURS,)), dma((COLOURS,)), dma((2,)), dma((2,)),
            pltpu.SemaphoreType.REGULAR((3,)),
        ],
        compiler_params=pltpu.CompilerParams(
            collective_id=0, has_side_effects=True, vmem_limit_bytes=67043328
        ),
    )(
        particles,
        projections,
        ctf_table,
        inv_noise.reshape(1, pixels),
        trig,
        candidates.T,
        defocus_bin.reshape(1, 16),
        line_slab,
        slab_owner.reshape(1, groups),
    )
    return (jnp.transpose(data, (0, 2, 1, 3))[None], jnp.transpose(weight, (1, 0, 2))[None])


def solution(mesh):
    return jax.shard_map(
        body,
        mesh=mesh,
        in_specs=(
            P(("grp", "dev"), None, None),
            P(("grp", "dev")),
            P(("grp", "dev"), None),
            P("dev", None, None),
            P(),
            P(),
            P("dev", None),
            P(),
        ),
        out_specs=(P("grp", "dev", None, None, None), P("grp", "dev", None, None)),
        check_vma=False,
    )
```

```python
import math

import jax
import jax.numpy as jnp
import numpy as np
from jax import lax
from jax.experimental import pallas as pl
from jax.experimental.pallas import tpu as pltpu
from jax.sharding import PartitionSpec as P

LINE = 128
CAP = 6
BINS = 16
NODES = 16
COLOURS = 2
CHUNKS = 4
ROWS = 8
NEG = -3.0e38
MESH = pl.DeviceIdType.MESH
F32 = jnp.float32
BF16 = jnp.bfloat16
HIGH = lax.Precision.HIGHEST
NN = (((1,), (0,)), ((), ()))
NT = (((1,), (1,)), ((), ()))
TN = (((0,), (0,)), ((), ()))
STAGES = (
    ((1, 4, 5), (3, 12, 15)),
    ((3, 12, 15), (1, 4, 5)),
)
NEAR = (1, 3, 4, 12, 5, 15)


def dot(a, b, dims=NN, precision=None):
    return lax.dot_general(a, b, dims, preferred_element_type=F32, precision=precision)


def phase_rows(lines):
    line = np.repeat(np.arange(lines), LINE).astype(np.float64)
    column = np.tile(np.arange(LINE), lines)
    freq = np.where(column < LINE // 2, column, column - LINE).astype(np.float64)
    moves = ((0, 1), (1, -1), (1, 0), (1, 1))
    angle = np.stack([dx * line + dy * freq for dx, dy in moves]) * (2.0 * math.pi / LINE)
    return np.concatenate([np.cos(angle), np.sin(angle)]).astype(np.float32)


def flip(v, k):
    if k == 0:
        return v
    if k == 1:
        return v + 1 - 2 * (v % 2)
    if k == 2:
        return (v + 2) % 4
    return 3 - v


def make_kernel(lines, groups):
    half = lines * LINE // 2
    width = half // COLOURS
    hl = lines // 2
    piece = half // CHUNKS
    slots = 32

    def kernel(parts, proj, table, noise, trig, cand, bins, slab, owner,
               o_data, o_weight,
               xin, xs, ctfv, candb, binb, slabv, owners, trigv, tabh, tabf, noisev, nsv, pbuf, ps, rbuf,
               gscr, bpscr, sx, cscr, bsscr, dbuf, rsb, zb, sel, wkey, w3, zsend, zrecv, wzs, wzr,
               loc, ex_s, ex_r, ag_s, ag_a, ag_b, ag_l, rs_s, rs_a, rs_b, sx_sem, zx_s, zx_r, z_sem, w_sem, ring):
        z = lax.axis_index("grp")
        d = lax.axis_index("dev")
        core = d % 2
        node = d // 2
        nx, ny = node % 4, node // 4
        other = 1 - core

        def dev(k, c):
            return (z, (flip(ny, k // 4) * 4 + flip(nx, k % 4)) * 2 + c)

        def along(k):
            return ((z + k + groups) % groups, d)

        mate = (z, node * 2 + other)

        def greet(sem, to):
            pl.semaphore_signal(sem, inc=1, device_id=to, device_id_type=MESH)

        barrier = pltpu.get_barrier_semaphore()
        greet(barrier, mate)
        for k in NEAR:
            greet(barrier, dev(k, core))
            greet(barrier, dev(k, other))
        greet(barrier, along(1))
        greet(barrier, along(-1))

        mine = pl.multiple_of(core * half, LINE)
        theirs = pl.multiple_of(other * half, LINE)
        loads = [
            pltpu.make_async_copy(bins, binb.at[core], loc.at[0]),
            pltpu.make_async_copy(table.at[:, pl.ds(mine, half)], tabh, loc.at[1]),
            pltpu.make_async_copy(parts.at[:, :, pl.ds(mine, half)], xin.at[core], loc.at[2]),
            pltpu.make_async_copy(trig.at[:, pl.ds(mine, half)], trigv, loc.at[3]),
            pltpu.make_async_copy(proj.at[:, :, pl.ds(mine, half)], pbuf.at[0, core], loc.at[4]),
            pltpu.make_async_copy(noise.at[:, pl.ds(mine, half)], noisev, loc.at[5]),
            pltpu.make_async_copy(cand, candb.at[core], loc.at[6]),
            pltpu.make_async_copy(slab, slabv, loc.at[7]),
            pltpu.make_async_copy(table, tabf, loc.at[8]),
            pltpu.make_async_copy(owner, owners, loc.at[9]),
        ]
        for c in loads:
            c.start()

        pl.semaphore_wait(barrier, 3 + 2 * len(NEAR))

        def span(q):
            return slice(q * width, (q + 1) * width)

        def cast(q, t, c):
            side = pl.multiple_of((mine if c is core else theirs) + q * width, LINE)
            return pltpu.make_async_remote_copy(
                src_ref=proj.at[:, :, pl.ds(side, width)],
                dst_ref=pbuf.at[t, core, :, :, span(q)],
                send_sem=ag_s.at[0],
                recv_sem=ag_a.at[q, STAGES[q][0].index(t)] if t in STAGES[q][0] else ag_b.at[q],
                device_id=dev(t, c), device_id_type=MESH,
            )

        def relay(q, k, s, t):
            return pltpu.make_async_remote_copy(
                src_ref=pbuf.at[k, s, :, :, span(q)], dst_ref=pbuf.at[k ^ t, s, :, :, span(q)],
                send_sem=ag_s.at[0], recv_sem=ag_l.at[q],
                device_id=dev(t, core), device_id_type=MESH,
            )

        def settle(ref, send, recv):
            return pltpu.make_async_remote_copy(
                src_ref=ref, dst_ref=ref, send_sem=send, recv_sem=recv, device_id=mate, device_id_type=MESH,
            )

        sent = []

        def push(c):
            c.start()
            sent.append(c)

        for stage in range(2):
            for i in (0, 1, 2):
                for q in range(COLOURS):
                    cast(q, STAGES[q][stage][i], core).start()
                    cast(q, STAGES[q][stage][i], other).start()
        swaps = [
            pltpu.make_async_remote_copy(
                src_ref=src, dst_ref=dst, send_sem=ex_s.at[i], recv_sem=ex_r.at[i],
                device_id=mate, device_id_type=MESH,
            )
            for i, (src, dst) in enumerate(
                (
                    (proj.at[:, :, pl.ds(theirs, half)], pbuf.at[0, core]),
                    (bins, binb.at[core]),
                    (cand, candb.at[core]),
                    (parts.at[:, :, pl.ds(theirs, half)], xin.at[core]),
                )
            )
        ]
        for c in swaps:
            push(c)
        reach = 1
        rounds = []
        while 2 * reach <= groups // 2:
            rounds.append(reach)
            reach *= 2
        if rounds:
            greet(ring.at[0], along(1))
            greet(ring.at[0], along(-1))

        def spread_word(i):
            if i < len(rounds):
                pl.semaphore_wait(ring.at[i], 2)
                if i + 1 < len(rounds):
                    greet(ring.at[i + 1], along(rounds[i + 1]))
                    greet(ring.at[i + 1], along(-rounds[i + 1]))

        even2, odd2 = pl.ds(0, 16, stride=2), pl.ds(1, 16, stride=2)
        bid = lax.broadcasted_iota(jnp.int32, (BINS, 16), 0)

        def rotate(s):
            hot = (bid == binb[s]).astype(F32).astype(BF16)
            ctfv[...] = dot(hot, tabh[...], TN)

            def chunk(i, carry):
                for t in range(piece // LINE):
                    at_ = pl.ds(pl.multiple_of(i * piece + t * LINE, LINE), LINE)
                    for p in range(16):
                        xs[t, 2 * p : 2 * p + 2, :] = xin[s, p, :, at_].astype(F32)
                    for part in range(2):
                        x = ctfv[:, at_] * xs[t, even2 if part == 0 else odd2, :]
                        r0 = pl.multiple_of(512 + part * 32 + s * 16, 16)
                        rbuf[pl.ds(r0, 16), at_] = x.astype(BF16)
                        for u in range(8):
                            r0 = pl.multiple_of(part * 256 + u * 32 + s * 16, 16)
                            rbuf[pl.ds(r0, 16), at_] = (x * trigv[u : u + 1, at_]).astype(BF16)
                return carry

            lax.fori_loop(0, CHUNKS, chunk, 0)

        for i in range(4):
            loads[i].wait()
        rotate(core)
        for i in range(3):
            for q in range(COLOURS):
                k = STAGES[q][0][i]
                settle(pbuf.at[k, :, :, :, span(q)], ag_s.at[0], ag_a.at[q, i]).wait_recv()
                for t in STAGES[q][1][::-1]:
                    for s in range(2):
                        relay(q, k, s, t).start()
        swaps[1].wait_recv()
        swaps[3].wait_recv()
        rotate(other)

        for i in range(4, 10):
            loads[i].wait()
        swaps[2].wait_recv()
        lanes = lax.broadcasted_iota(jnp.int32, (1, 128), 1)
        cid = lax.broadcasted_iota(jnp.int32, (128, 128), 0)
        lane_core = (lanes % 32) // 16
        til = (
            lax.broadcasted_iota(jnp.int32, (16, 128), 1) % 16
            == lax.broadcasted_iota(jnp.int32, (16, 128), 0)
        ).astype(F32)
        bl = [dot(binb[s].astype(F32), til) for s in range(2)]
        blane = jnp.where(lane_core == 1, bl[1], bl[0]).astype(jnp.int32)
        ohb = (cid == blane).astype(F32)
        cl = [dot(candb[s].astype(F32), til) for s in range(2)]
        clane = jnp.where(lane_core == 1, cl[1], cl[0]).astype(jnp.int32)
        rid = lax.broadcasted_iota(jnp.int32, (64, 128), 0)
        jid = ((rid // 4) ^ node) * 4 + rid % 4
        listed = jid == clane[0:1, :]
        for k in range(1, 8):
            listed = jnp.logical_or(listed, jid == clane[k : k + 1, :])
        t32 = tabh[...].astype(F32)
        ns32 = t32 * t32 * noisev[...]
        ns_hi = ns32.astype(BF16)
        nsv[0:BINS, :] = ns_hi
        nsv[BINS : 2 * BINS, :] = (ns32 - ns_hi.astype(F32)).astype(BF16)
        bpscr[...] = jnp.zeros(bpscr.shape, F32)
        gscr[...] = jnp.zeros(gscr.shape, F32)

        def score(q, ks):
            for i, k in enumerate(ks):
                for s in range(2):
                    for j in range(2):
                        r = 8 * i + 4 * s + 2 * j
                        ps[r : r + 2, :] = pbuf[k, s, j, :, span(q)].astype(F32)
            p32 = ps[0 : 8 * len(ks), :]
            nz = noisev[:, span(q)]
            got = dot((p32 * nz).astype(BF16), rbuf[:, span(q)], NT)
            pp = p32 * p32
            pp_hi = pp.astype(BF16)
            pp_lo = (pp - pp_hi.astype(F32)).astype(BF16)
            ns = nsv[:, span(q)]
            power = dot(pp_hi, ns, NT)
            power = power[:, 0:BINS] + power[:, BINS : 2 * BINS] + dot(pp_lo, ns[0:BINS], NT)
            for i, k in enumerate(ks):
                here, there = slice(8 * i, 8 * i + 8), slice(8 * k, 8 * k + 8)
                bpscr[there, 0:BINS] += power[here, :]
                for b in range(5):
                    w = min(128, 576 - 128 * b)
                    gscr[b, there, 0:w] += got[here, 128 * b : 128 * b + w]

        swaps[0].wait_recv()
        for q in range(COLOURS):
            settle(pbuf.at[1:4, :, :, :, span(q)], ag_s.at[0], ag_b.at[q]).wait_recv()
            score(q, (0,) + STAGES[q][0] + STAGES[q][1])
        spread_word(0)
        for q in range(COLOURS):
            late = tuple(a ^ b for a in STAGES[q][0] for b in STAGES[q][1])
            settle(pbuf.at[1:10, :, :, :, span(q)], ag_s.at[0], ag_l.at[q]).wait_recv()
            score(q, late)
        even, odd = pl.ds(0, 64, stride=2), pl.ds(1, 64, stride=2)
        ge = [gscr[k, even, :] for k in range(5)]
        go = [gscr[k, odd, :] for k in range(5)]
        sx[core, 0] = ge[0] + go[2]
        sx[core, 1] = go[1] - ge[3]
        sx[core, 2] = jnp.where(
            lanes < 32, ge[4] + pltpu.roll(go[4], 96, 1), pltpu.roll(bpscr[even, :] + bpscr[odd, :], 64, 1)
        )
        trade = pltpu.make_async_remote_copy(
            src_ref=sx.at[core], dst_ref=sx.at[core], send_sem=sx_sem.at[0], recv_sem=sx_sem.at[1],
            device_id=mate, device_id_type=MESH,
        )
        push(trade)
        spread_word(1)
        trade.wait_recv()

        last = sx[0, 2] + sx[1, 2]
        power = jnp.where(lanes < BINS, pltpu.roll(last, 64, 1), 0.0)
        quad = 0.5 * dot(power, ohb, NN, HIGH)
        base = sx[0, 0] + sx[1, 0] - quad
        turn = sx[0, 1] + sx[1, 1]
        first = jnp.logical_and(listed, lanes < 32)
        s_plus = jnp.where(listed, base - turn, NEG)
        s_minus = jnp.where(listed, base + turn, NEG)
        s_zero = jnp.where(first, last - quad, NEG)
        peak = jnp.max(jnp.maximum(jnp.maximum(s_plus, s_minus), s_zero), axis=0, keepdims=True)
        peak = jnp.maximum(peak, pltpu.roll(peak, 32, 1))
        peak = jnp.maximum(peak, pltpu.roll(peak, 64, 1))
        e_plus = jnp.where(listed, jnp.exp(s_plus - peak), 0.0)
        e_minus = jnp.where(listed, jnp.exp(s_minus - peak), 0.0)
        e_zero = jnp.where(first, jnp.exp(s_zero - peak), 0.0)
        total = jnp.sum(e_plus + e_minus + e_zero, axis=0, keepdims=True)
        total = total + pltpu.roll(total, 32, 1)
        total = total + pltpu.roll(total, 64, 1)
        inv = 1.0 / total
        both = (e_plus + e_minus) * inv
        gap = (e_plus - e_minus) * inv
        zero = e_zero * inv
        blank = jnp.zeros((64, 128), F32)
        for k, (a, b) in enumerate(
            ((both, blank), (blank, -gap), (blank, both), (gap, blank), (zero, pltpu.roll(zero, 32, 1)))
        ):
            cscr[k, even, :] = a
            cscr[k, odd, :] = b
        coef = jnp.concatenate([cscr[k] for k in range(5)], axis=1)[:, 0:576].astype(BF16)

        def rspan(q):
            return slice(q * width, (q + 1) * width + (128 if q == COLOURS - 1 else 0))

        def rs(q, k, t):
            return pltpu.make_async_remote_copy(
                src_ref=dbuf.at[k, :, rspan(q)], dst_ref=rsb.at[k, :, rspan(q)],
                send_sem=rs_s.at[0],
                recv_sem=rs_b.at[q] if k == t else rs_a.at[q, STAGES[q][0].index(k ^ t)],
                device_id=dev(t, core), device_id_type=MESH,
            )

        def collect(q, k, froms):
            acc = dbuf[k, :, rspan(q)].astype(F32)
            arrival = rs_a.at[q, STAGES[q][0].index(k)] if k else rs_b.at[q]
            settle(rsb.at[1 : 1 + len(froms), :, rspan(q)], rs_s.at[0], arrival).wait_recv()
            for child in froms:
                acc = acc + rsb[child, :, rspan(q)].astype(F32)
            return acc

        for q in range(COLOURS):
            if q == COLOURS - 1:
                share = dot(both + zero, ohb, NT, HIGH)
                bsscr[even, :] = share
                bsscr[odd, :] = blank
                dbuf[:, :, half : half + 128] = bsscr[...].reshape(NODES, ROWS, 128).astype(BF16)
            out = dot(coef, rbuf[:, span(q)])
            dbuf[:, :, span(q)] = out.reshape(NODES, ROWS, width).astype(BF16)
            for k in STAGES[q][0][::-1] + (0,):
                for t in STAGES[q][1][::-1]:
                    rs(q, k ^ t, t).start()

        lid = lax.broadcasted_iota(jnp.int32, (groups, lines), 0)
        tri = (
            lax.broadcasted_iota(jnp.int32, (lines, lines), 0)
            < lax.broadcasted_iota(jnp.int32, (lines, lines), 1)
        ).astype(F32)
        place = lax.broadcasted_iota(jnp.int32, (lines, lines * ROWS), 1) // ROWS
        place = jnp.where(place < hl, place + core * hl, place - core * hl)
        wide = (place == lax.broadcasted_iota(jnp.int32, (lines, lines * ROWS), 0)).astype(F32)
        wide16 = (
            lax.broadcasted_iota(jnp.int32, (lines, lines * BINS), 1) // BINS
            == lax.broadcasted_iota(jnp.int32, (lines, lines * BINS), 0)
        ).astype(F32)
        keys = []
        for j in range(2):
            row = slabv[j : j + 1, :]
            own = jnp.zeros((1, lines), jnp.int32)
            for s in range(groups):
                own = own + jnp.where(row == s, owners[0, s], 0)
            hit = (lid == own).astype(F32)
            rank = jnp.sum(hit * dot(hit, tri), axis=0, keepdims=True)
            keys.append((own * 8).astype(F32) + rank)
        key8 = [dot(k, wide) for k in keys]
        col = lax.broadcasted_iota(jnp.int32, (1, lines * ROWS), 1) % ROWS
        pick = jnp.where(col % 4 >= 2, key8[1], key8[0]).astype(jnp.int32) * 8 + col
        rid = lax.broadcasted_iota(jnp.int32, (groups * slots, lines * ROWS), 0)
        inner = rid % slots
        r4 = (
            (inner >= CAP).astype(jnp.int32)
            + (inner >= 2 * CAP).astype(jnp.int32)
            + (inner >= 3 * CAP).astype(jnp.int32)
            + (inner >= 4 * CAP).astype(jnp.int32)
        )
        want = ((rid // slots) * 8 + (inner - CAP * r4)) * 8 + 4 * core + r4
        sel[...] = (want == pick).astype(F32).astype(BF16)
        for j in range(2):
            wkey[8 * j : 8 * j + 8, :] = jnp.broadcast_to(dot(keys[j], wide16), (8, lines * BINS))

        for i in (2, 1, 0):
            for q in range(COLOURS):
                k = STAGES[q][0][i]
                acc = collect(q, k, [k ^ t for t in STAGES[q][1]])
                dbuf[k, :, rspan(q)] = acc.astype(BF16)
                rs(q, k, k).start()

        def squares(i, carry):
            v = tabf[:, pl.ds(pl.multiple_of(i * LINE, LINE), LINE)].astype(F32)
            w3[pl.ds(pl.multiple_of(i * BINS, BINS), BINS), :] = v * v
            return carry

        lax.fori_loop(0, lines, squares, 0)
        spread_word(2)
        def zx(q):
            return pltpu.make_async_remote_copy(
                src_ref=zb.at[core, :, span(q)], dst_ref=zb.at[core, :, span(q)],
                send_sem=zx_s.at[q], recv_sem=zx_r.at[q], device_id=mate, device_id_type=MESH,
            )

        extra = None
        for q in range(COLOURS):
            acc = collect(q, 0, STAGES[q][1] + STAGES[q][0])
            zb[core, :, span(q)] = acc[:, :width].astype(BF16)
            push(zx(q))
            if q == COLOURS - 1:
                extra = acc[:, width:]

        rows8 = lax.broadcasted_iota(jnp.int32, (8, 128), 0)
        for j in range(2):
            wzs[j : j + 1, :] = jnp.sum(
                jnp.where(rows8 == 4 * core + 2 * j, extra, 0.0), axis=0, keepdims=True
            )
        order = sorted(range(1, groups), key=lambda k: -min(k, groups - k))

        def wmsg(k):
            return pltpu.make_async_remote_copy(
                src_ref=wzs, dst_ref=wzr.at[k], send_sem=w_sem.at[0], recv_sem=w_sem.at[1],
                device_id=((z + k) % groups, d), device_id_type=MESH,
            )

        def zmsg(k):
            return pltpu.make_async_remote_copy(
                src_ref=zsend.at[(z + k) % groups, 0 : 4 * CAP], dst_ref=zrecv.at[k, 0 : 4 * CAP],
                send_sem=z_sem.at[0], recv_sem=z_sem.at[1],
                device_id=((z + k) % groups, d), device_id_type=MESH,
            )

        for k in order:
            wmsg(k).start()
        def stack(h):
            return jnp.concatenate(
                [zb[h, :, LINE * i : LINE * i + LINE].astype(F32) for i in range(hl)], axis=0
            ).astype(BF16)

        packed = dot(sel[:, 0 : hl * ROWS], stack(core))
        for q in range(COLOURS):
            zx(q).wait_recv()
        packed = packed + dot(sel[:, hl * ROWS :], stack(other))
        zsend[...] = packed.astype(BF16).reshape(groups, slots, LINE)
        for k in order:
            zmsg(k).start()
        acc_w = wzs[...]
        settle(wzr.at[1:groups], w_sem.at[0], w_sem.at[1]).wait_recv()
        for k in range(1, groups):
            acc_w = acc_w + wzr[k]
        spread = (
            lax.broadcasted_iota(jnp.int32, (128, lines * BINS), 1) % BINS
            == lax.broadcasted_iota(jnp.int32, (128, lines * BINS), 0)
        ).astype(F32)
        scale = 64.0 / (16 * groups * NODES * 2)
        tall = jnp.concatenate(
            [jnp.broadcast_to(acc_w[j : j + 1, :] * scale, (8, 128)) for j in range(2)], axis=0
        )
        coefw = dot(tall, spread, NN, HIGH)
        slot = lax.broadcasted_iota(jnp.int32, (16, lines * BINS), 0) % 8
        ok = wkey[...].astype(jnp.int32) == z * 8 + slot
        weights = dot(jnp.where(ok, coefw, 0.0), w3[...], NN, HIGH)
        for j in range(2):
            for c in range(CAP):
                o_weight[c, j : j + 1, :] = weights[8 * j + c : 8 * j + c + 1, :]
        acc = zsend[z, 0 : 4 * CAP].astype(F32)
        settle(zrecv.at[1:groups, 0 : 4 * CAP], z_sem.at[0], z_sem.at[1]).wait_recv()
        for k in range(1, groups):
            acc = acc + zrecv[k, 0 : 4 * CAP].astype(F32)
        for r in range(4):
            for c in range(CAP):
                o_data[r // 2, c, r % 2 : r % 2 + 1, :] = acc[CAP * r + c : CAP * r + c + 1, :]

        for c in sent:
            c.wait_send()
        settle(pbuf.at[1:NODES], ag_s.at[0], ag_l.at[0]).wait_send()
        settle(dbuf.at[1:NODES], rs_s.at[0], rs_b.at[0]).wait_send()
        settle(wzr.at[1:groups], w_sem.at[0], w_sem.at[1]).wait_send()
        settle(zrecv.at[1:groups, 0 : 4 * CAP], z_sem.at[0], z_sem.at[1]).wait_send()

    return kernel


def body(particles, defocus_bin, candidates, projections, ctf_table, inv_noise, line_slab, slab_owner):
    groups = lax.axis_size("grp")
    pixels = particles.shape[2]
    lines = pixels // LINE
    half = pixels // 2
    trig = jnp.asarray(phase_rows(lines))
    hbm = pl.BlockSpec(memory_space=pltpu.HBM)
    vmem = pl.BlockSpec(memory_space=pltpu.VMEM)
    dma = pltpu.SemaphoreType.DMA
    data, weight = pl.pallas_call(
        make_kernel(lines, groups),
        name="estep",
        out_shape=(
            jax.ShapeDtypeStruct((2, CAP, 2, LINE), F32),
            jax.ShapeDtypeStruct((CAP, 2, LINE), F32),
        ),
        in_specs=[hbm] * 9,
        out_specs=(vmem, vmem),
        scratch_shapes=[
            pltpu.VMEM((2, 16, 2, half), BF16),
            pltpu.VMEM((half // CHUNKS // LINE, 32, LINE), F32),
            pltpu.VMEM((16, half), F32),
            pltpu.VMEM((2, 8, 16), jnp.int32),
            pltpu.VMEM((2, 1, 16), jnp.int32),
            pltpu.VMEM((2, lines), jnp.int32),
            pltpu.SMEM((1, groups), jnp.int32),
            pltpu.VMEM((8, half), F32),
            pltpu.VMEM((BINS, half), BF16),
            pltpu.VMEM((BINS, pixels), BF16),
            pltpu.VMEM((1, half), F32),
            pltpu.VMEM((2 * BINS, half), BF16),
            pltpu.VMEM((NODES, 2, 2, 2, half), BF16),
            pltpu.VMEM((128, half // COLOURS), F32),
            pltpu.VMEM((576, half), BF16),
            pltpu.VMEM((5, 128, 128), F32),
            pltpu.VMEM((128, 128), F32),
            pltpu.VMEM((2, 3, 64, 128), F32),
            pltpu.VMEM((5, 128, 128), F32),
            pltpu.VMEM((128, 128), F32),
            pltpu.VMEM((NODES, ROWS, half + 128), BF16),
            pltpu.VMEM((NODES, ROWS, half + 128), BF16),
            pltpu.VMEM((2, ROWS, half), BF16),
            pltpu.VMEM((groups * 32, lines * ROWS), BF16),
            pltpu.VMEM((16, lines * BINS), F32),
            pltpu.VMEM((lines * BINS, LINE), F32),
            pltpu.VMEM((groups, 32, LINE), BF16),
            pltpu.VMEM((groups, 32, LINE), BF16),
            pltpu.VMEM((2, 128), F32),
            pltpu.VMEM((groups, 2, 128), F32),
            dma((10,)), dma((4,)), dma((4,)),
            dma((1,)), dma((COLOURS, 3)), dma((COLOURS,)), dma((COLOURS,)),
            dma((1,)), dma((COLOURS, 3)), dma((COLOURS,)),
            dma((2,)), dma((COLOURS,)), dma((COLOURS,)), dma((2,)), dma((2,)),
            pltpu.SemaphoreType.REGULAR((3,)),
        ],
        compiler_params=pltpu.CompilerParams(
            collective_id=0, has_side_effects=True, vmem_limit_bytes=67043328
        ),
    )(
        particles,
        projections,
        ctf_table,
        inv_noise.reshape(1, pixels),
        trig,
        candidates.T,
        defocus_bin.reshape(1, 16),
        line_slab,
        slab_owner.reshape(1, groups),
    )
    return (jnp.transpose(data, (0, 2, 1, 3))[None], jnp.transpose(weight, (1, 0, 2))[None])


def solution(mesh):
    return jax.shard_map(
        body,
        mesh=mesh,
        in_specs=(
            P(("grp", "dev"), None, None),
            P(("grp", "dev")),
            P(("grp", "dev"), None),
            P("dev", None, None),
            P(),
            P(),
            P("dev", None),
            P(),
        ),
        out_specs=(P("grp", "dev", None, None, None), P("grp", "dev", None, None)),
        check_vma=False,
    )
```

```python
import math

import jax
import jax.numpy as jnp
import numpy as np
from jax import lax
from jax.experimental import pallas as pl
from jax.experimental.pallas import tpu as pltpu
from jax.sharding import PartitionSpec as P

LINE = 128
CAP = 6
BINS = 16
NODES = 16
COLOURS = 2
CHUNKS = 4
ROWS = 8
NEG = -3.0e38
MESH = pl.DeviceIdType.MESH
F32 = jnp.float32
BF16 = jnp.bfloat16
HIGH = lax.Precision.HIGHEST
NN = (((1,), (0,)), ((), ()))
NT = (((1,), (1,)), ((), ()))
TN = (((0,), (0,)), ((), ()))
STAGES = (
    ((1, 4, 5), (3, 12, 15)),
    ((3, 12, 15), (1, 4, 5)),
)
NEAR = (1, 3, 4, 12, 5, 15)


def dot(a, b, dims=NN, precision=None):
    return lax.dot_general(a, b, dims, preferred_element_type=F32, precision=precision)


def phase_rows(lines):
    line = np.repeat(np.arange(lines), LINE).astype(np.float64)
    column = np.tile(np.arange(LINE), lines)
    freq = np.where(column < LINE // 2, column, column - LINE).astype(np.float64)
    moves = ((0, 1), (1, -1), (1, 0), (1, 1))
    angle = np.stack([dx * line + dy * freq for dx, dy in moves]) * (2.0 * math.pi / LINE)
    return np.concatenate([np.cos(angle), np.sin(angle)]).astype(np.float32)


def flip(v, k):
    if k == 0:
        return v
    if k == 1:
        return v + 1 - 2 * (v % 2)
    if k == 2:
        return (v + 2) % 4
    return 3 - v


def make_kernel(lines, groups):
    half = lines * LINE // 2
    width = half // COLOURS
    hl = lines // 2
    piece = half // CHUNKS
    slots = 32

    def kernel(parts, proj, table, noise, trig, cand, bins, slab, owner,
               o_data, o_weight,
               xin, xs, ctfv, candb, binb, slabv, owners, trigv, tabh, tabf, noisev, nsv, pbuf, ps, rbuf,
               gscr, bpscr, sx, cscr, bsscr, dbuf, rsb, zb, sel, wkey, w3, zsend, zrecv, wzs, wzr,
               loc, ex_s, ex_r, ag_s, ag_a, ag_b, ag_l, rs_s, rs_a, rs_b, sx_sem, zx_s, zx_r, z_sem, w_sem, ring):
        z = lax.axis_index("grp")
        d = lax.axis_index("dev")
        core = d % 2
        node = d // 2
        nx, ny = node % 4, node // 4
        other = 1 - core

        def dev(k, c):
            return (z, (flip(ny, k // 4) * 4 + flip(nx, k % 4)) * 2 + c)

        def along(k):
            return ((z + k + groups) % groups, d)

        mate = (z, node * 2 + other)

        def greet(sem, to):
            pl.semaphore_signal(sem, inc=1, device_id=to, device_id_type=MESH)

        barrier = pltpu.get_barrier_semaphore()
        greet(barrier, mate)
        for k in NEAR:
            greet(barrier, dev(k, core))
            greet(barrier, dev(k, other))
        greet(barrier, along(1))
        greet(barrier, along(-1))

        mine = pl.multiple_of(core * half, LINE)
        theirs = pl.multiple_of(other * half, LINE)
        loads = [
            pltpu.make_async_copy(bins, binb.at[core], loc.at[0]),
            pltpu.make_async_copy(table.at[:, pl.ds(mine, half)], tabh, loc.at[1]),
            pltpu.make_async_copy(parts.at[:, :, pl.ds(mine, half)], xin.at[core], loc.at[2]),
            pltpu.make_async_copy(trig.at[:, pl.ds(mine, half)], trigv, loc.at[3]),
            pltpu.make_async_copy(proj.at[:, :, pl.ds(mine, half)], pbuf.at[0, core], loc.at[4]),
            pltpu.make_async_copy(noise.at[:, pl.ds(mine, half)], noisev, loc.at[5]),
            pltpu.make_async_copy(cand, candb.at[core], loc.at[6]),
            pltpu.make_async_copy(slab, slabv, loc.at[7]),
            pltpu.make_async_copy(table, tabf, loc.at[8]),
            pltpu.make_async_copy(owner, owners, loc.at[9]),
        ]
        for c in loads:
            c.start()

        pl.semaphore_wait(barrier, 3 + 2 * len(NEAR))

        def span(q):
            return slice(q * width, (q + 1) * width)

        def cast(q, t, c):
            side = pl.multiple_of((mine if c is core else theirs) + q * width, LINE)
            return pltpu.make_async_remote_copy(
                src_ref=proj.at[:, :, pl.ds(side, width)],
                dst_ref=pbuf.at[t, core, :, :, span(q)],
                send_sem=ag_s.at[0],
                recv_sem=ag_a.at[q, STAGES[q][0].index(t)] if t in STAGES[q][0] else ag_b.at[q],
                device_id=dev(t, c), device_id_type=MESH,
            )

        def relay(q, k, s, t):
            return pltpu.make_async_remote_copy(
                src_ref=pbuf.at[k, s, :, :, span(q)], dst_ref=pbuf.at[k ^ t, s, :, :, span(q)],
                send_sem=ag_s.at[0], recv_sem=ag_l.at[q],
                device_id=dev(t, core), device_id_type=MESH,
            )

        def settle(ref, send, recv):
            return pltpu.make_async_remote_copy(
                src_ref=ref, dst_ref=ref, send_sem=send, recv_sem=recv, device_id=mate, device_id_type=MESH,
            )

        sent = []

        def push(c):
            c.start()
            sent.append(c)

        for stage in range(2):
            for i in (1, 0, 2):
                for q in range(COLOURS):
                    cast(q, STAGES[q][stage][i], core).start()
                    cast(q, STAGES[q][stage][i], other).start()
        swaps = [
            pltpu.make_async_remote_copy(
                src_ref=src, dst_ref=dst, send_sem=ex_s.at[i], recv_sem=ex_r.at[i],
                device_id=mate, device_id_type=MESH,
            )
            for i, (src, dst) in enumerate(
                (
                    (proj.at[:, :, pl.ds(theirs, half)], pbuf.at[0, core]),
                    (bins, binb.at[core]),
                    (cand, candb.at[core]),
                    (parts.at[:, :, pl.ds(theirs, half)], xin.at[core]),
                )
            )
        ]
        for c in swaps:
            push(c)
        reach = 1
        rounds = []
        while 2 * reach <= groups // 2:
            rounds.append(reach)
            reach *= 2
        if rounds:
            greet(ring.at[0], along(1))
            greet(ring.at[0], along(-1))

        def spread_word(i):
            if i < len(rounds):
                pl.semaphore_wait(ring.at[i], 2)
                if i + 1 < len(rounds):
                    greet(ring.at[i + 1], along(rounds[i + 1]))
                    greet(ring.at[i + 1], along(-rounds[i + 1]))

        even2, odd2 = pl.ds(0, 16, stride=2), pl.ds(1, 16, stride=2)
        bid = lax.broadcasted_iota(jnp.int32, (BINS, 16), 0)

        def rotate(s):
            hot = (bid == binb[s]).astype(F32).astype(BF16)
            ctfv[...] = dot(hot, tabh[...], TN)

            def chunk(i, carry):
                for t in range(piece // LINE):
                    at_ = pl.ds(pl.multiple_of(i * piece + t * LINE, LINE), LINE)
                    for p in range(16):
                        xs[t, 2 * p : 2 * p + 2, :] = xin[s, p, :, at_].astype(F32)
                    for part in range(2):
                        x = ctfv[:, at_] * xs[t, even2 if part == 0 else odd2, :]
                        r0 = pl.multiple_of(512 + part * 32 + s * 16, 16)
                        rbuf[pl.ds(r0, 16), at_] = x.astype(BF16)
                        for u in range(8):
                            r0 = pl.multiple_of(part * 256 + u * 32 + s * 16, 16)
                            rbuf[pl.ds(r0, 16), at_] = (x * trigv[u : u + 1, at_]).astype(BF16)
                return carry

            lax.fori_loop(0, CHUNKS, chunk, 0)

        for i in range(4):
            loads[i].wait()
        rotate(core)
        for i in range(3):
            for q in range(COLOURS):
                k = STAGES[q][0][i]
                settle(pbuf.at[k, :, :, :, span(q)], ag_s.at[0], ag_a.at[q, i]).wait_recv()
                for t in STAGES[q][1][::-1]:
                    for s in range(2):
                        relay(q, k, s, t).start()
        swaps[1].wait_recv()
        swaps[3].wait_recv()
        rotate(other)

        for i in range(4, 10):
            loads[i].wait()
        swaps[2].wait_recv()
        lanes = lax.broadcasted_iota(jnp.int32, (1, 128), 1)
        cid = lax.broadcasted_iota(jnp.int32, (128, 128), 0)
        lane_core = (lanes % 32) // 16
        til = (
            lax.broadcasted_iota(jnp.int32, (16, 128), 1) % 16
            == lax.broadcasted_iota(jnp.int32, (16, 128), 0)
        ).astype(F32)
        bl = [dot(binb[s].astype(F32), til) for s in range(2)]
        blane = jnp.where(lane_core == 1, bl[1], bl[0]).astype(jnp.int32)
        ohb = (cid == blane).astype(F32)
        cl = [dot(candb[s].astype(F32), til) for s in range(2)]
        clane = jnp.where(lane_core == 1, cl[1], cl[0]).astype(jnp.int32)
        rid = lax.broadcasted_iota(jnp.int32, (64, 128), 0)
        jid = ((rid // 4) ^ node) * 4 + rid % 4
        listed = jid == clane[0:1, :]
        for k in range(1, 8):
            listed = jnp.logical_or(listed, jid == clane[k : k + 1, :])
        t32 = tabh[...].astype(F32)
        ns32 = t32 * t32 * noisev[...]
        ns_hi = ns32.astype(BF16)
        nsv[0:BINS, :] = ns_hi
        nsv[BINS : 2 * BINS, :] = (ns32 - ns_hi.astype(F32)).astype(BF16)
        bpscr[...] = jnp.zeros(bpscr.shape, F32)
        gscr[...] = jnp.zeros(gscr.shape, F32)

        def score(q, ks):
            for i, k in enumerate(ks):
                for s in range(2):
                    for j in range(2):
                        r = 8 * i + 4 * s + 2 * j
                        ps[r : r + 2, :] = pbuf[k, s, j, :, span(q)].astype(F32)
            p32 = ps[0 : 8 * len(ks), :]
            nz = noisev[:, span(q)]
            got = dot((p32 * nz).astype(BF16), rbuf[:, span(q)], NT)
            pp = p32 * p32
            pp_hi = pp.astype(BF16)
            pp_lo = (pp - pp_hi.astype(F32)).astype(BF16)
            ns = nsv[:, span(q)]
            power = dot(pp_hi, ns, NT)
            power = power[:, 0:BINS] + power[:, BINS : 2 * BINS] + dot(pp_lo, ns[0:BINS], NT)
            for i, k in enumerate(ks):
                here, there = slice(8 * i, 8 * i + 8), slice(8 * k, 8 * k + 8)
                bpscr[there, 0:BINS] += power[here, :]
                for b in range(5):
                    w = min(128, 576 - 128 * b)
                    gscr[b, there, 0:w] += got[here, 128 * b : 128 * b + w]

        swaps[0].wait_recv()
        for q in range(COLOURS):
            settle(pbuf.at[1:4, :, :, :, span(q)], ag_s.at[0], ag_b.at[q]).wait_recv()
            score(q, (0,) + STAGES[q][0] + STAGES[q][1])
        spread_word(0)
        for q in range(COLOURS):
            late = tuple(a ^ b for a in STAGES[q][0] for b in STAGES[q][1])
            settle(pbuf.at[1:10, :, :, :, span(q)], ag_s.at[0], ag_l.at[q]).wait_recv()
            score(q, late)
        even, odd = pl.ds(0, 64, stride=2), pl.ds(1, 64, stride=2)
        ge = [gscr[k, even, :] for k in range(5)]
        go = [gscr[k, odd, :] for k in range(5)]
        sx[core, 0] = ge[0] + go[2]
        sx[core, 1] = go[1] - ge[3]
        sx[core, 2] = jnp.where(
            lanes < 32, ge[4] + pltpu.roll(go[4], 96, 1), pltpu.roll(bpscr[even, :] + bpscr[odd, :], 64, 1)
        )
        trade = pltpu.make_async_remote_copy(
            src_ref=sx.at[core], dst_ref=sx.at[core], send_sem=sx_sem.at[0], recv_sem=sx_sem.at[1],
            device_id=mate, device_id_type=MESH,
        )
        push(trade)
        spread_word(1)
        trade.wait_recv()

        last = sx[0, 2] + sx[1, 2]
        power = jnp.where(lanes < BINS, pltpu.roll(last, 64, 1), 0.0)
        quad = 0.5 * dot(power, ohb, NN, HIGH)
        base = sx[0, 0] + sx[1, 0] - quad
        turn = sx[0, 1] + sx[1, 1]
        first = jnp.logical_and(listed, lanes < 32)
        s_plus = jnp.where(listed, base - turn, NEG)
        s_minus = jnp.where(listed, base + turn, NEG)
        s_zero = jnp.where(first, last - quad, NEG)
        peak = jnp.max(jnp.maximum(jnp.maximum(s_plus, s_minus), s_zero), axis=0, keepdims=True)
        peak = jnp.maximum(peak, pltpu.roll(peak, 32, 1))
        peak = jnp.maximum(peak, pltpu.roll(peak, 64, 1))
        e_plus = jnp.where(listed, jnp.exp(s_plus - peak), 0.0)
        e_minus = jnp.where(listed, jnp.exp(s_minus - peak), 0.0)
        e_zero = jnp.where(first, jnp.exp(s_zero - peak), 0.0)
        total = jnp.sum(e_plus + e_minus + e_zero, axis=0, keepdims=True)
        total = total + pltpu.roll(total, 32, 1)
        total = total + pltpu.roll(total, 64, 1)
        inv = 1.0 / total
        both = (e_plus + e_minus) * inv
        gap = (e_plus - e_minus) * inv
        zero = e_zero * inv
        blank = jnp.zeros((64, 128), F32)
        for k, (a, b) in enumerate(
            ((both, blank), (blank, -gap), (blank, both), (gap, blank), (zero, pltpu.roll(zero, 32, 1)))
        ):
            cscr[k, even, :] = a
            cscr[k, odd, :] = b
        coef = jnp.concatenate([cscr[k] for k in range(5)], axis=1)[:, 0:576].astype(BF16)

        def rspan(q):
            return slice(q * width, (q + 1) * width + (128 if q == COLOURS - 1 else 0))

        def rs(q, k, t):
            return pltpu.make_async_remote_copy(
                src_ref=dbuf.at[k, :, rspan(q)], dst_ref=rsb.at[k, :, rspan(q)],
                send_sem=rs_s.at[0],
                recv_sem=rs_b.at[q] if k == t else rs_a.at[q, STAGES[q][0].index(k ^ t)],
                device_id=dev(t, core), device_id_type=MESH,
            )

        def collect(q, k, froms):
            acc = dbuf[k, :, rspan(q)].astype(F32)
            arrival = rs_a.at[q, STAGES[q][0].index(k)] if k else rs_b.at[q]
            settle(rsb.at[1 : 1 + len(froms), :, rspan(q)], rs_s.at[0], arrival).wait_recv()
            for child in froms:
                acc = acc + rsb[child, :, rspan(q)].astype(F32)
            return acc

        for q in range(COLOURS):
            if q == COLOURS - 1:
                share = dot(both + zero, ohb, NT, HIGH)
                bsscr[even, :] = share
                bsscr[odd, :] = blank
                dbuf[:, :, half : half + 128] = bsscr[...].reshape(NODES, ROWS, 128).astype(BF16)
            out = dot(coef, rbuf[:, span(q)])
            dbuf[:, :, span(q)] = out.reshape(NODES, ROWS, width).astype(BF16)
            for k in STAGES[q][0][::-1] + (0,):
                for t in STAGES[q][1][::-1]:
                    rs(q, k ^ t, t).start()

        lid = lax.broadcasted_iota(jnp.int32, (groups, lines), 0)
        tri = (
            lax.broadcasted_iota(jnp.int32, (lines, lines), 0)
            < lax.broadcasted_iota(jnp.int32, (lines, lines), 1)
        ).astype(F32)
        place = lax.broadcasted_iota(jnp.int32, (lines, lines * ROWS), 1) // ROWS
        place = jnp.where(place < hl, place + core * hl, place - core * hl)
        wide = (place == lax.broadcasted_iota(jnp.int32, (lines, lines * ROWS), 0)).astype(F32)
        wide16 = (
            lax.broadcasted_iota(jnp.int32, (lines, lines * BINS), 1) // BINS
            == lax.broadcasted_iota(jnp.int32, (lines, lines * BINS), 0)
        ).astype(F32)
        keys = []
        for j in range(2):
            row = slabv[j : j + 1, :]
            own = jnp.zeros((1, lines), jnp.int32)
            for s in range(groups):
                own = own + jnp.where(row == s, owners[0, s], 0)
            hit = (lid == own).astype(F32)
            rank = jnp.sum(hit * dot(hit, tri), axis=0, keepdims=True)
            keys.append((own * 8).astype(F32) + rank)
        key8 = [dot(k, wide) for k in keys]
        col = lax.broadcasted_iota(jnp.int32, (1, lines * ROWS), 1) % ROWS
        pick = jnp.where(col % 4 >= 2, key8[1], key8[0]).astype(jnp.int32) * 8 + col
        rid = lax.broadcasted_iota(jnp.int32, (groups * slots, lines * ROWS), 0)
        inner = rid % slots
        r4 = (
            (inner >= CAP).astype(jnp.int32)
            + (inner >= 2 * CAP).astype(jnp.int32)
            + (inner >= 3 * CAP).astype(jnp.int32)
            + (inner >= 4 * CAP).astype(jnp.int32)
        )
        want = ((rid // slots) * 8 + (inner - CAP * r4)) * 8 + 4 * core + r4
        sel[...] = (want == pick).astype(F32).astype(BF16)
        for j in range(2):
            wkey[8 * j : 8 * j + 8, :] = jnp.broadcast_to(dot(keys[j], wide16), (8, lines * BINS))

        for i in (2, 1, 0):
            for q in range(COLOURS):
                k = STAGES[q][0][i]
                acc = collect(q, k, [k ^ t for t in STAGES[q][1]])
                dbuf[k, :, rspan(q)] = acc.astype(BF16)
                rs(q, k, k).start()

        def squares(i, carry):
            v = tabf[:, pl.ds(pl.multiple_of(i * LINE, LINE), LINE)].astype(F32)
            w3[pl.ds(pl.multiple_of(i * BINS, BINS), BINS), :] = v * v
            return carry

        lax.fori_loop(0, lines, squares, 0)
        spread_word(2)
        def zx(q):
            return pltpu.make_async_remote_copy(
                src_ref=zb.at[core, :, span(q)], dst_ref=zb.at[core, :, span(q)],
                send_sem=zx_s.at[q], recv_sem=zx_r.at[q], device_id=mate, device_id_type=MESH,
            )

        extra = None
        for q in range(COLOURS):
            acc = collect(q, 0, STAGES[q][1] + STAGES[q][0])
            zb[core, :, span(q)] = acc[:, :width].astype(BF16)
            push(zx(q))
            if q == COLOURS - 1:
                extra = acc[:, width:]

        rows8 = lax.broadcasted_iota(jnp.int32, (8, 128), 0)
        for j in range(2):
            wzs[j : j + 1, :] = jnp.sum(
                jnp.where(rows8 == 4 * core + 2 * j, extra, 0.0), axis=0, keepdims=True
            )
        order = sorted(range(1, groups), key=lambda k: -min(k, groups - k))

        def wmsg(k):
            return pltpu.make_async_remote_copy(
                src_ref=wzs, dst_ref=wzr.at[k], send_sem=w_sem.at[0], recv_sem=w_sem.at[1],
                device_id=((z + k) % groups, d), device_id_type=MESH,
            )

        def zmsg(k):
            return pltpu.make_async_remote_copy(
                src_ref=zsend.at[(z + k) % groups, 0 : 4 * CAP], dst_ref=zrecv.at[k, 0 : 4 * CAP],
                send_sem=z_sem.at[0], recv_sem=z_sem.at[1],
                device_id=((z + k) % groups, d), device_id_type=MESH,
            )

        for k in order:
            wmsg(k).start()
        def stack(h):
            return jnp.concatenate(
                [zb[h, :, LINE * i : LINE * i + LINE].astype(F32) for i in range(hl)], axis=0
            ).astype(BF16)

        packed = dot(sel[:, 0 : hl * ROWS], stack(core))
        for q in range(COLOURS):
            zx(q).wait_recv()
        packed = packed + dot(sel[:, hl * ROWS :], stack(other))
        zsend[...] = packed.astype(BF16).reshape(groups, slots, LINE)
        for k in order:
            zmsg(k).start()
        acc_w = wzs[...]
        settle(wzr.at[1:groups], w_sem.at[0], w_sem.at[1]).wait_recv()
        for k in range(1, groups):
            acc_w = acc_w + wzr[k]
        spread = (
            lax.broadcasted_iota(jnp.int32, (128, lines * BINS), 1) % BINS
            == lax.broadcasted_iota(jnp.int32, (128, lines * BINS), 0)
        ).astype(F32)
        scale = 64.0 / (16 * groups * NODES * 2)
        tall = jnp.concatenate(
            [jnp.broadcast_to(acc_w[j : j + 1, :] * scale, (8, 128)) for j in range(2)], axis=0
        )
        coefw = dot(tall, spread, NN, HIGH)
        slot = lax.broadcasted_iota(jnp.int32, (16, lines * BINS), 0) % 8
        ok = wkey[...].astype(jnp.int32) == z * 8 + slot
        weights = dot(jnp.where(ok, coefw, 0.0), w3[...], NN, HIGH)
        for j in range(2):
            for c in range(CAP):
                o_weight[c, j : j + 1, :] = weights[8 * j + c : 8 * j + c + 1, :]
        acc = zsend[z, 0 : 4 * CAP].astype(F32)
        settle(zrecv.at[1:groups, 0 : 4 * CAP], z_sem.at[0], z_sem.at[1]).wait_recv()
        for k in range(1, groups):
            acc = acc + zrecv[k, 0 : 4 * CAP].astype(F32)
        for r in range(4):
            for c in range(CAP):
                o_data[r // 2, c, r % 2 : r % 2 + 1, :] = acc[CAP * r + c : CAP * r + c + 1, :]

        for c in sent:
            c.wait_send()
        settle(pbuf.at[1:NODES], ag_s.at[0], ag_l.at[0]).wait_send()
        settle(dbuf.at[1:NODES], rs_s.at[0], rs_b.at[0]).wait_send()
        settle(wzr.at[1:groups], w_sem.at[0], w_sem.at[1]).wait_send()
        settle(zrecv.at[1:groups, 0 : 4 * CAP], z_sem.at[0], z_sem.at[1]).wait_send()

    return kernel


def body(particles, defocus_bin, candidates, projections, ctf_table, inv_noise, line_slab, slab_owner):
    groups = lax.axis_size("grp")
    pixels = particles.shape[2]
    lines = pixels // LINE
    half = pixels // 2
    trig = jnp.asarray(phase_rows(lines))
    hbm = pl.BlockSpec(memory_space=pltpu.HBM)
    vmem = pl.BlockSpec(memory_space=pltpu.VMEM)
    dma = pltpu.SemaphoreType.DMA
    data, weight = pl.pallas_call(
        make_kernel(lines, groups),
        name="estep",
        out_shape=(
            jax.ShapeDtypeStruct((2, CAP, 2, LINE), F32),
            jax.ShapeDtypeStruct((CAP, 2, LINE), F32),
        ),
        in_specs=[hbm] * 9,
        out_specs=(vmem, vmem),
        scratch_shapes=[
            pltpu.VMEM((2, 16, 2, half), BF16),
            pltpu.VMEM((half // CHUNKS // LINE, 32, LINE), F32),
            pltpu.VMEM((16, half), F32),
            pltpu.VMEM((2, 8, 16), jnp.int32),
            pltpu.VMEM((2, 1, 16), jnp.int32),
            pltpu.VMEM((2, lines), jnp.int32),
            pltpu.SMEM((1, groups), jnp.int32),
            pltpu.VMEM((8, half), F32),
            pltpu.VMEM((BINS, half), BF16),
            pltpu.VMEM((BINS, pixels), BF16),
            pltpu.VMEM((1, half), F32),
            pltpu.VMEM((2 * BINS, half), BF16),
            pltpu.VMEM((NODES, 2, 2, 2, half), BF16),
            pltpu.VMEM((128, half // COLOURS), F32),
            pltpu.VMEM((576, half), BF16),
            pltpu.VMEM((5, 128, 128), F32),
            pltpu.VMEM((128, 128), F32),
            pltpu.VMEM((2, 3, 64, 128), F32),
            pltpu.VMEM((5, 128, 128), F32),
            pltpu.VMEM((128, 128), F32),
            pltpu.VMEM((NODES, ROWS, half + 128), BF16),
            pltpu.VMEM((NODES, ROWS, half + 128), BF16),
            pltpu.VMEM((2, ROWS, half), BF16),
            pltpu.VMEM((groups * 32, lines * ROWS), BF16),
            pltpu.VMEM((16, lines * BINS), F32),
            pltpu.VMEM((lines * BINS, LINE), F32),
            pltpu.VMEM((groups, 32, LINE), BF16),
            pltpu.VMEM((groups, 32, LINE), BF16),
            pltpu.VMEM((2, 128), F32),
            pltpu.VMEM((groups, 2, 128), F32),
            dma((10,)), dma((4,)), dma((4,)),
            dma((1,)), dma((COLOURS, 3)), dma((COLOURS,)), dma((COLOURS,)),
            dma((1,)), dma((COLOURS, 3)), dma((COLOURS,)),
            dma((2,)), dma((COLOURS,)), dma((COLOURS,)), dma((2,)), dma((2,)),
            pltpu.SemaphoreType.REGULAR((3,)),
        ],
        compiler_params=pltpu.CompilerParams(
            collective_id=0, has_side_effects=True, vmem_limit_bytes=67043328
        ),
    )(
        particles,
        projections,
        ctf_table,
        inv_noise.reshape(1, pixels),
        trig,
        candidates.T,
        defocus_bin.reshape(1, 16),
        line_slab,
        slab_owner.reshape(1, groups),
    )
    return (jnp.transpose(data, (0, 2, 1, 3))[None], jnp.transpose(weight, (1, 0, 2))[None])


def solution(mesh):
    return jax.shard_map(
        body,
        mesh=mesh,
        in_specs=(
            P(("grp", "dev"), None, None),
            P(("grp", "dev")),
            P(("grp", "dev"), None),
            P("dev", None, None),
            P(),
            P(),
            P("dev", None),
            P(),
        ),
        out_specs=(P("grp", "dev", None, None, None), P("grp", "dev", None, None)),
        check_vma=False,
    )
```
